32 devices in a mesh: batch: 8 (over y, x, core), tile: 4 (over z).
Axes of the slice: x: 2, y: 2, z: 4, core: 2. Of those that a mesh axis runs over, the one named last changes fastest.
Arguments:
- object_field: float32 [2, 2, 3072, 1536], P(None, None, 'batch', 'tile'), may hold values from -6 to 6
- probe_wave: bfloat16 [2, 256, 256], replicated, may hold values from -4.1875 to 4.1875
- intensities: float32 [512, 256, 256], P(('batch', 'tile')), may hold values from 0 to 4
- owner_rows: int32 [512, 1], P(('batch', 'tile')), may hold values from 0 to 7; in each aligned block of 16 rows (0 to 15, 16 to 31, ...) at most 4 rows name the same one
- offsets: int32 [512, 2], P(('batch', 'tile')), may hold values from 0 to 128
Outputs:
- new_object: float32 [2, 2, 3072, 1536], P(None, None, 'batch', 'tile')
- new_probe: float32 [2, 256, 256], replicated
The draws below stay inside these ranges and needn't reach their ends.
Inputs may be any that keep to these rules, and one draw needn't show every extreme that they name: `owner_rows`: within the 16 positions of one device, each tile row is named at most 4 times.
All inputs are finite; a program needn't handle non-finite values.
Results may differ from the reference program's by a relative error of at most 0.008.
The reference program's roundings to bfloat16 on the way count: a program that leaves them out, or rounds other values in their place, can miss the bound.
Values may be sent and summed in bfloat16 or wider, within the bound.
A program may use at most 192 MiB of HBM per device.

```python
import math
import jax
import jax.numpy as jnp
import numpy as np
from jax import lax

W = 256
S = 2
TS = 384
P_DEV = 16
CAP = 4
POSITIONS = 512
NY = 3072
NX = 1536
N_BATCH = 8
N_TILE = 4


def set_ends(result, rng, least, largest):
    spot = [jax.random.randint(jax.random.fold_in(rng, axis), (), 0, length) for axis, length in enumerate(result.shape)]
    main_axis = result.shape.index(max(result.shape))
    neighbour = spot[:main_axis] + [(spot[main_axis] + 1) % result.shape[main_axis]] + spot[main_axis + 1:]
    return result.at[tuple(spot)].set(least).at[tuple(neighbour)].set(largest)


def shard_levels(rng, dims, cuts, least, top_value):
    def one(dim, shards_of):
        draws = jax.random.uniform(jax.random.fold_in(jax.random.fold_in(rng, 6), dim), (shards_of,), jnp.float32, least / len(cuts), top_value / len(cuts))
        return jnp.repeat(jnp.exp(draws), dims[dim] // shards_of).reshape((-1,) + (1,) * (len(dims) - dim - 1))

    level = one(*cuts[0])
    for cut in cuts[1:]:
        level = level * one(*cut)
    return level


def assign_block(own_key, own, number, rows, count, top, limit, skew):
    sequence = jax.random.permutation(own_key, count)
    packed, usual = load_shares(count, rows * top, limit, skew, True), load_shares(count, rows * top, limit, skew, False)
    places = jnp.arange(count)

    def named(lengths, rotation):
        used = int((lengths > 0).sum())
        fixed = max(1, used // 4)
        shifted = fixed + (places - fixed + rotation * (used - fixed)) % max(1, count - fixed)
        return jnp.zeros((count,), jnp.int32).at[sequence[jnp.where(places < fixed, places, shifted)]].set(jnp.asarray(lengths, jnp.int32))

    lengths = jnp.where(number % 4 == 0, named(packed, number // 4), named(usual, number - number // 4 - 1))
    mixed = jax.random.permutation(jax.random.fold_in(own, 3), count)
    giver, sink = mixed[0:count // 2 * 2:2], mixed[1:count // 2 * 2:2]
    room = jnp.minimum(lengths[giver] - 1, limit - lengths[sink]) // 2
    room = jnp.where((giver == sequence[0]) | (sink == sequence[0]) | (lengths[sink] == 0), 0, jnp.maximum(room, 0))
    shifted = jax.random.randint(jax.random.fold_in(own, 4), (count // 2,), 0, 1 << 20) % (room + 1)
    lengths = lengths.at[giver].add(-shifted).at[sink].add(shifted)
    members = jnp.searchsorted(jnp.cumsum(lengths), jnp.arange(rows * top), side="right").astype(jnp.int32)
    grid = members.reshape(top, rows).T
    grid = grid[jax.random.permutation(jax.random.fold_in(own, 1), rows)]
    rotation = jax.random.randint(jax.random.fold_in(own, 2), (rows, 1), 0, top)
    return jnp.take_along_axis(grid, (jnp.arange(top)[None, :] + rotation) % top, axis=1)


def load_shares(number_of, total, bound, slope, full):
    portions = [(1 << 20) // math.isqrt(standing ** slope) + 1 for standing in range(1, number_of + 1)]
    largest = bound if full else min(bound, max(-(-total // number_of), total * portions[0] // sum(portions)))
    least = 1 if total - largest >= number_of - 1 else 0
    given, spare = [largest] + [least] * (number_of - 1), total - largest - least * (number_of - 1)
    while spare > 0:
        free = [i for i in range(1, number_of) if given[i] < largest] or [i for i in range(1, number_of) if given[i] < bound]
        pool, remaining = sum([portions[i] for i in free]), spare
        for i in free:
            addition = min(bound - given[i], max(1, remaining * portions[i] // pool), spare)
            given[i] = given[i] + addition
            spare = spare - addition
    return np.array(given)


def normal_values(key, dims, scale, reach, cuts=(), held_as=jnp.bfloat16):
    drawn = jax.random.normal(key, dims, jnp.float32) * scale
    if len(cuts) > 0:
        drawn = shard_levels(key, dims, cuts, -0.22, 0.18) * drawn
    return jnp.clip(drawn, min=-reach, max=reach).astype(held_as)


def setup_inputs(seed: int = 0) -> dict:
    streams_of = jax.random.split(jax.random.key(seed), 6)
    object_field = normal_values(streams_of[0], (S, 2, NY, NX), 1.0, 6.0, ((2, 8), (3, 4)), jnp.float32)
    probe_wave = normal_values(streams_of[1], (2, W, W), 0.7, 4.1875)
    intensities = jnp.clip(4.0 * jax.random.uniform(streams_of[2], (POSITIONS, W, W), jnp.float32) ** shard_levels(streams_of[2], (POSITIONS, W, W), ((0, 32),), -0.2, 0.2), 0.0, 4.0)
    owner_rows_keys = jax.random.split(jax.random.fold_in(streams_of[3], 1), POSITIONS // P_DEV)
    owner_rows_turns = jax.random.permutation(jax.random.fold_in(streams_of[3], 3), POSITIONS // P_DEV)
    owner_rows = jax.vmap(lambda own, number: assign_block(jax.random.fold_in(streams_of[3], 2), own, number, P_DEV, N_BATCH, 1, CAP, 2))(owner_rows_keys, owner_rows_turns).reshape((POSITIONS, 1))
    offsets = set_ends(jax.random.randint(streams_of[4], (POSITIONS, 2), 0, TS - W + 1), jax.random.fold_in(streams_of[4], 1), 0, TS - W).astype(jnp.int32)
    return {"object_field": object_field, "probe_wave": probe_wave, "intensities": intensities, "owner_rows": owner_rows, "offsets": offsets}


update_rate = 0.1
tv_weight = 12.0
tv_smooth = 1.0
probe_rate = 0.04

def tables(extent):
    counter = jnp.arange(extent, dtype=jnp.int32)
    product = counter[:, None] * counter[None, :] % extent
    angles = product.astype(jnp.float32) * (2.0 * math.pi / extent)
    scaling = 1.0 / math.sqrt(extent)
    cos_table = (jnp.cos(angles) * scaling).astype(jnp.bfloat16)
    sin_table = (-jnp.sin(angles) * scaling).astype(jnp.bfloat16)
    frequency = (counter + extent // 2) % extent - extent // 2
    squared = (frequency * frequency).astype(jnp.float32)
    phases = -(0.5 / extent) * (squared[:, None] + squared[None, :])
    return (cos_table, sin_table, jnp.cos(phases), jnp.sin(phases))

def transform(real_part, imag_part, cos_table, sin_table):
    extent = real_part.shape[0]
    left_stack = jnp.concatenate([cos_table, sin_table], 0)
    right_stack = jnp.concatenate([real_part, imag_part], 1)
    blocks = jnp.dot(left_stack, right_stack, preferred_element_type=jnp.float32)
    mid_real = (blocks[:extent, :extent] - blocks[extent:, extent:]).astype(jnp.bfloat16)
    mid_imag = (blocks[:extent, extent:] + blocks[extent:, :extent]).astype(jnp.bfloat16)
    left_two = jnp.concatenate([mid_real, mid_imag], 0)
    right_two = jnp.concatenate([cos_table, sin_table], 1)
    second = jnp.dot(left_two, right_two, preferred_element_type=jnp.float32)
    out_real = second[:extent, :extent] - second[extent:, extent:]
    out_imag = second[:extent, extent:] + second[extent:, :extent]
    return (out_real, out_imag)

def multislice(object_patch, probe_wave, measured, cos_table, sin_table, prop_real, prop_imag):
    slices = object_patch.shape[0]
    back_sin = -sin_table
    psi_real = probe_wave[0]
    psi_imag = probe_wave[1]
    entering = []
    for slab_index in range(slices):
        trans_real = object_patch[slab_index, 0].astype(jnp.float32)
        trans_imag = object_patch[slab_index, 1].astype(jnp.float32)
        entering.append((psi_real, psi_imag))
        wave_real = psi_real.astype(jnp.float32)
        wave_imag = psi_imag.astype(jnp.float32)
        prod_real = (wave_real * trans_real - wave_imag * trans_imag).astype(jnp.bfloat16)
        prod_imag = (wave_real * trans_imag + wave_imag * trans_real).astype(jnp.bfloat16)
        if slab_index + 1 < slices:
            far_real, far_imag = transform(prod_real, prod_imag, cos_table, sin_table)
            kick_real = (prop_real * far_real - prop_imag * far_imag).astype(jnp.bfloat16)
            kick_imag = (prop_real * far_imag + prop_imag * far_real).astype(jnp.bfloat16)
            near_real, near_imag = transform(kick_real, kick_imag, cos_table, back_sin)
            psi_real = near_real.astype(jnp.bfloat16)
            psi_imag = near_imag.astype(jnp.bfloat16)
    exit_real, exit_imag = transform(prod_real, prod_imag, cos_table, sin_table)
    misfit = 0.5 * (exit_real * exit_real + exit_imag * exit_imag - measured)
    chi_real = (misfit * exit_real).astype(jnp.bfloat16)
    chi_imag = (misfit * exit_imag).astype(jnp.bfloat16)
    grad_real, grad_imag = transform(chi_real, chi_imag, cos_table, back_sin)
    object_grads = [None] * slices
    for slab_index in reversed(range(slices)):
        trans_real = object_patch[slab_index, 0].astype(jnp.float32)
        trans_imag = object_patch[slab_index, 1].astype(jnp.float32)
        wave_real = entering[slab_index][0].astype(jnp.float32)
        wave_imag = entering[slab_index][1].astype(jnp.float32)
        object_grads[slab_index] = jnp.stack([grad_real * wave_real + grad_imag * wave_imag, grad_imag * wave_real - grad_real * wave_imag])
        dpsi_real = grad_real * trans_real + grad_imag * trans_imag
        dpsi_imag = grad_imag * trans_real - grad_real * trans_imag
        if slab_index > 0:
            back_real, back_imag = transform(dpsi_real.astype(jnp.bfloat16), dpsi_imag.astype(jnp.bfloat16), cos_table, back_sin)
            turn_real = (prop_real * back_real + prop_imag * back_imag).astype(jnp.bfloat16)
            turn_imag = (prop_real * back_imag - prop_imag * back_real).astype(jnp.bfloat16)
            grad_real, grad_imag = transform(turn_real, turn_imag, cos_table, sin_table)
    patch_grad = jnp.stack(object_grads).astype(jnp.bfloat16)
    probe_grad = jnp.stack([dpsi_real, dpsi_imag])
    return (patch_grad, probe_grad)

def tv_gradient(field):
    down_diff = jnp.roll(field, -1, axis=2) - field
    right_diff = jnp.roll(field, -1, axis=3) - field
    weight = 1.0 / jnp.sqrt(lax.optimization_barrier(jnp.sum(down_diff * down_diff + right_diff * right_diff, axis=1, keepdims=True)) + tv_smooth)
    flow_down = weight * down_diff
    flow_right = weight * right_diff
    return jnp.roll(flow_down, 1, axis=2) + jnp.roll(flow_right, 1, axis=3) - flow_down - flow_right

def reference(object_field, probe_wave, intensities, owner_rows, offsets):
    cos_table, sin_table, prop_real, prop_imag = tables(W)
    total_rows = intensities.shape[0]
    serial = jnp.arange(total_rows, dtype=jnp.int32)
    columns = serial // P_DEV % N_TILE
    row_start = (owner_rows[:, 0] * TS + offsets[:, 0]).astype(jnp.int32)
    col_start = (columns * TS + offsets[:, 1]).astype(jnp.int32)
    anchor = jnp.zeros((), jnp.int32)

    def visit_one(state_in, inputs):
        field_grad, probe_total = state_in
        measured, row_at, col_at = inputs
        start = (anchor, anchor, row_at, col_at)
        object_patch = lax.dynamic_slice(object_field, start, (S, 2, W, W)).astype(jnp.bfloat16)
        patch_grad, probe_grad = multislice(object_patch, probe_wave, measured, cos_table, sin_table, prop_real, prop_imag)
        current = lax.dynamic_slice(field_grad, start, (S, 2, W, W))
        field_grad = lax.dynamic_update_slice(field_grad, current + patch_grad.astype(jnp.float32), start)
        return ((field_grad, probe_total + probe_grad), None)
    initial = (jnp.zeros(object_field.shape, jnp.float32), jnp.zeros((2, W, W), jnp.float32))
    (field_grad, probe_total), _ = lax.scan(visit_one, initial, (intensities, row_start, col_start))
    new_object = object_field - update_rate * (field_grad + tv_weight * tv_gradient(object_field))
    new_probe = probe_wave.astype(jnp.float32) - probe_rate * probe_total
    return (new_object, new_probe)
```

```python
import math

import jax
import jax.numpy as jnp
from jax import lax
from jax.experimental import pallas as pl
from jax.experimental.pallas import tpu as pltpu
from jax.sharding import PartitionSpec as P

update_rate = 0.1
tv_weight = 12.0
tv_smooth = 1.0
probe_rate = 0.04
lanes = 128
fields = 4
tail_rows = 16
f32, bf16 = jnp.float32, jnp.bfloat16


def extended(x, sides, width):
    for axis, dim in sides:
        size, length = (lax.axis_size(axis), x.shape[dim])
        up = [(i, (i + 1) % size) for i in range(size)]
        down = [(j, i) for i, j in up]
        last = lax.slice_in_dim(x, length - width, length, axis=dim)
        first = lax.slice_in_dim(x, 0, width, axis=dim)
        before = lax.ppermute(last, axis, up)
        after = lax.ppermute(first, axis, down)
        x = jnp.concatenate([before, x, after], axis=dim)
    return x


def tables(extent):
    half = extent // 2
    counter = jnp.arange(extent, dtype=jnp.int32)
    product = counter[:, None] * counter[None, :] % extent
    angles = product.astype(f32) * (2.0 * math.pi / extent)
    scaling = 1.0 / math.sqrt(extent)
    cos_table = (jnp.cos(angles) * scaling).astype(bf16)
    sin_table = (-jnp.sin(angles) * scaling).astype(bf16)

    def packed(first):
        real, imag = cos_table[first::2, :half], sin_table[first::2, :half]
        return jnp.concatenate(
            [jnp.concatenate([real, -imag], 1), jnp.concatenate([imag, real], 1)], 0
        )

    even, odd = packed(0), packed(1)
    frequency = (counter + half) % extent - half
    frequency = jnp.concatenate([frequency[0::2], frequency[1::2]])
    squared = (frequency * frequency).astype(f32)
    phases = -(0.5 / extent) * (squared[:, None] + squared[None, :])
    order = jnp.concatenate([counter[0::2], counter[1::2]])
    sort = (counter[:, None] == order[None, :]).astype(bf16)
    return (
        jnp.stack([even, odd, even.T, odd.T]),
        jnp.stack([jnp.cos(phases), jnp.sin(phases)]),
        sort,
    )


def dot(a, b):
    return jnp.dot(a, b, preferred_element_type=f32)


def outward(real, imag, even, odd, even_t, odd_t):
    half = real.shape[0] // 2
    near = [(x[:half] + x[half:]).astype(bf16) for x in (real, imag)]
    far = [(x[:half] - x[half:]).astype(bf16) for x in (real, imag)]
    a = dot(even, jnp.concatenate(near, 0))
    b = dot(odd, jnp.concatenate(far, 0))

    def both(x, sign):
        y = (x[:, :half] + sign * x[:, half:]).astype(bf16)
        return jnp.concatenate([y[:half], y[half:]], 1)

    ye = dot(jnp.concatenate([both(a, 1), both(b, 1)], 0), even_t)
    yo = dot(jnp.concatenate([both(a, -1), both(b, -1)], 0), odd_t)
    return (
        jnp.concatenate([ye[:, :half], yo[:, :half]], 1),
        jnp.concatenate([ye[:, half:], yo[:, half:]], 1),
    )


def inward(real, imag, even, odd, even_t, odd_t):
    half = real.shape[0] // 2
    e = dot(even_t, jnp.concatenate([real[:half], imag[:half]], 0))
    o = dot(odd_t, jnp.concatenate([real[half:], imag[half:]], 0))
    p = (e + o).astype(bf16)
    m = (e - o).astype(bf16)

    def cut(at):
        return jnp.concatenate(
            [
                jnp.concatenate([x[:half, at : at + half], x[half:, at : at + half]], 1)
                for x in (p, m)
            ],
            0,
        )

    ye = dot(cut(0), even)
    yo = dot(cut(half), odd)
    p = ye + yo
    m = ye - yo
    return (
        jnp.concatenate([p[:, :half], m[:, :half]], 1),
        jnp.concatenate([p[:, half:], m[:, half:]], 1),
    )


def visit(
    tile, row_at, col_at, measured, probe_ref, tables_ref, prop_ref, wide, summed, total, psi, trans
):
    slices, extent = psi.shape[0], psi.shape[-1]
    half = extent // 2
    rest = lax.rem(col_at, lanes)
    base = lax.div(col_at, lanes)
    rows = pl.ds(row_at, extent)
    back = lax.rem(lanes - rest, lanes)
    lane = lax.broadcasted_iota(jnp.int32, (extent, lanes), 1)
    keep = lane < lanes - rest
    ahead = lane >= rest
    args = tuple(tables_ref[i] for i in range(4))
    last = wide.shape[3] - 1
    spots = [jnp.minimum(base + j, last) for j in range(3)]

    def entering(slab):
        if slab == 0:
            return probe_ref[0].astype(f32), probe_ref[1].astype(f32)
        return psi[slab, 0].astype(f32), psi[slab, 1].astype(f32)

    for slab in range(slices):
        for part in range(2):
            cols = [
                pltpu.roll(wide[tile, slab, part, spots[j], rows, :], back, 1) for j in range(3)
            ]
            trans[slab, part, :, :half] = jnp.where(keep, cols[0], cols[1])
            trans[slab, part, :, half:] = jnp.where(keep, cols[1], cols[2])
    for slab in range(slices):
        wr, wi = entering(slab)
        tr, ti = trans[slab, 0], trans[slab, 1]
        fr, fi = outward(wr * tr - wi * ti, wr * ti + wi * tr, *args)
        if slab + 1 < slices:
            pr, pi = prop_ref[0], prop_ref[1]
            nr, ni = inward(
                (pr * fr - pi * fi).astype(bf16), (pr * fi + pi * fr).astype(bf16), *args
            )
            psi[slab + 1, 0] = nr.astype(bf16)
            psi[slab + 1, 1] = ni.astype(bf16)
    misfit = 0.5 * (fr * fr + fi * fi - measured)
    gr, gi = inward((misfit * fr).astype(bf16), (misfit * fi).astype(bf16), *args)

    def add(slab, part, value):
        value = value.astype(bf16).astype(f32)
        left = pltpu.roll(value[:, :half], rest, 1)
        right = pltpu.roll(value[:, half:], rest, 1)
        summed[tile, slab, part, spots[0], rows, :] += jnp.where(ahead, left, 0.0)
        summed[tile, slab, part, spots[1], rows, :] += jnp.where(ahead, right, left)
        summed[tile, slab, part, spots[2], rows, :] += jnp.where(ahead, 0.0, right)

    for slab in reversed(range(slices)):
        wr, wi = entering(slab)
        tr, ti = trans[slab, 0], trans[slab, 1]
        add(slab, 0, gr * wr + gi * wi)
        add(slab, 1, gi * wr - gr * wi)
        qr = gr * tr + gi * ti
        qi = gi * tr - gr * ti
        if slab > 0:
            bi, br = outward(qi, qr, *args)
            pr, pi = prop_ref[0], prop_ref[1]
            ur = (pr * br + pi * bi).astype(bf16)
            ui = (pr * bi - pi * br).astype(bf16)
            gi, gr = inward(ui, ur, *args)
    total[0] += qr
    total[1] += qi


def visits_kernel(cap, first, sources, *refs):
    pays = refs[:sources]
    own_ref, other_ref, probe_ref, tables_ref, prop_ref = refs[sources : sources + 5]
    carried = refs[sources + 5 : sources + 5 + (0 if first else 2)]
    sums_ref, total_ref, wide, psi, trans, notes, plan, sem = refs[sources + 5 + len(carried) :]
    extent = probe_ref.shape[-1]
    for s, pay in enumerate(pays):
        notes[s * 8 : s * 8 + 8] = pay[cap * extent :, :lanes].astype(f32)[:8].astype(jnp.int32)
    copy = pltpu.make_async_copy(notes, plan, sem)
    copy.start()
    for t, tile_ref in enumerate((own_ref, other_ref)):
        for s in range(tile_ref.shape[0]):
            for p in range(2):
                for j in range(wide.shape[3]):
                    wide[t, s, p, j] = tile_ref[s, p, :, j * lanes : (j + 1) * lanes].astype(f32)
    if first:
        sums_ref[...] = jnp.zeros_like(sums_ref)
        total_ref[...] = jnp.zeros_like(total_ref)
    else:
        sums_ref[...] = carried[0][...]
        total_ref[...] = carried[1][...]
    copy.wait()
    for s, pay in enumerate(pays):

        def body(i, carry, s=s, pay=pay):
            note = [plan[s * 8, i * fields + k] for k in range(fields)]

            @pl.when(note[0] > 0)
            def _():
                measured = pay[pl.ds(pl.multiple_of(i * extent, extent), extent), :].astype(f32)
                visit(
                    note[1], note[2], note[3], measured, probe_ref, tables_ref, prop_ref,
                    wide, sums_ref, total_ref, psi, trans,
                )

            return carry

        lax.fori_loop(0, cap, body, 0)


def visits(cap, pays, own, other, probe, fixed, carried):
    tabs, prop, _ = fixed
    slices, _, tile_rows, tile_cols = own.shape
    extent = probe.shape[-1]
    sources = len(pays)
    block = (2, slices, 2, tile_cols // lanes, tile_rows, lanes)
    vmem = pl.BlockSpec(memory_space=pltpu.VMEM)

    def kernel(*refs):
        visits_kernel(cap, not carried, sources, *refs)

    operands = (*pays, own, other, probe, tabs, prop, *carried)
    return pl.pallas_call(
        kernel,
        in_specs=[vmem] * len(operands),
        out_specs=(vmem, vmem),
        out_shape=(
            jax.ShapeDtypeStruct(block, f32),
            jax.ShapeDtypeStruct((2, extent, extent), f32),
        ),
        scratch_shapes=[
            pltpu.VMEM(block, f32),
            pltpu.VMEM((slices, 2, extent, extent), bf16),
            pltpu.VMEM((slices, 2, extent, extent), f32),
            pltpu.VMEM((8 * sources, lanes), jnp.int32),
            pltpu.SMEM((8 * sources, lanes), jnp.int32),
            pltpu.SemaphoreType.DMA,
        ],
        compiler_params=pltpu.CompilerParams(vmem_limit_bytes=48 * 1024 * 1024),
        cost_estimate=pl.CostEstimate(
            flops=sources * cap * 3 * slices * 16 * extent**3,
            bytes_accessed=16 * 1024 * 1024,
            transcendentals=0,
        ),
    )(*operands)


def pack_kernel(cap, nbatch, owner_ref, offset_ref, measured_ref, field_ref, sort_ref, *refs):
    pays, (tile_ref, index, count) = refs[:nbatch], refs[nbatch:]
    positions, extent = measured_ref.shape[0], measured_ref.shape[-1]
    me = lax.axis_index("batch")

    def clear(i, carry):
        index[i] = -1
        return carry

    lax.fori_loop(0, nbatch * cap, clear, 0)

    def clear_count(i, carry):
        count[i] = 0
        return carry

    lax.fori_loop(0, nbatch, clear_count, 0)

    def place(p, carry):
        row = owner_ref[p, 0]
        rank = count[row]
        count[row] = rank + 1
        bit = lax.rem(row, 2)
        dest = row - bit + lax.rem(rank + row + me, 2)
        slot = bit * (cap // 2) + lax.div(rank, 2)
        index[jnp.bitwise_xor(dest, me) * cap + slot] = p
        return carry

    lax.fori_loop(0, positions, place, 0)
    lane = lax.broadcasted_iota(jnp.int32, (tail_rows, extent), 1)
    for mask, pay in enumerate(pays):
        dest_bit = lax.rem(jnp.bitwise_xor(me, mask), 2)
        tail = jnp.zeros((tail_rows, extent), jnp.int32)
        for slot in range(cap):
            p = index[mask * cap + slot]
            at = jnp.maximum(p, 0)
            bit = slot // (cap // 2)
            note = (
                jnp.where(p >= 0, 1, 0),
                jnp.where(dest_bit == bit, 0, 1),
                offset_ref[at, 0],
                offset_ref[at, 1],
            )
            for k, value in enumerate(note):
                tail = jnp.where(lane == slot * fields + k, value, tail)
        pay[cap * extent :, :] = tail.astype(f32).astype(bf16)

        def fill(slot, carry, mask=mask, pay=pay):
            p = index[mask * cap + slot]

            @pl.when(p >= 0)
            def _():
                sort = sort_ref[...]
                across = dot(measured_ref[p].astype(bf16), sort).astype(bf16)
                sorted_ = dot(sort.T, across)
                pay[pl.ds(pl.multiple_of(slot * extent, extent), extent), :] = sorted_.astype(bf16)

            return carry

        lax.fori_loop(0, cap, fill, 0)
    tile_ref[...] = field_ref[...].astype(bf16)


def pack(cap, owner_rows, offsets, intensities, field, sort):
    nbatch = lax.axis_size("batch")
    extent = intensities.shape[-1]
    smem = pl.BlockSpec(memory_space=pltpu.SMEM)
    vmem = pl.BlockSpec(memory_space=pltpu.VMEM)

    def kernel(*refs):
        pack_kernel(cap, nbatch, *refs)

    return pl.pallas_call(
        kernel,
        in_specs=[smem, smem, vmem, vmem, vmem],
        out_specs=[vmem] * (nbatch + 1),
        out_shape=[jax.ShapeDtypeStruct((cap * extent + tail_rows, extent), bf16)] * nbatch
        + [jax.ShapeDtypeStruct(field.shape, bf16)],
        scratch_shapes=[
            pltpu.SMEM((nbatch * cap,), jnp.int32),
            pltpu.SMEM((nbatch,), jnp.int32),
        ],
        compiler_params=pltpu.CompilerParams(vmem_limit_bytes=32 * 1024 * 1024),
    )(owner_rows, offsets, intensities, field, sort)


def tv_local(padded):
    corner_cells = padded[:, :, :-1, :-1]
    down_diff = padded[:, :, 1:, :-1] - corner_cells
    right_diff = padded[:, :, :-1, 1:] - corner_cells
    weight = 1.0 / jnp.sqrt(
        jnp.sum(down_diff * down_diff + right_diff * right_diff, axis=1, keepdims=True) + tv_smooth
    )
    flow_down = weight * down_diff
    flow_right = weight * right_diff
    return (
        flow_down[:, :, :-1, 1:]
        + flow_right[:, :, 1:, :-1]
        - flow_down[:, :, 1:, 1:]
        - flow_right[:, :, 1:, 1:]
    )


def on_device(object_field, probe_wave, intensities, owner_rows, offsets):
    extent = probe_wave.shape[-1]
    nbatch = lax.axis_size("batch")
    cap = max(2, 2 * intensities.shape[0] // nbatch)
    fixed = tables(extent)

    def swap(x, mask):
        return lax.ppermute(x, "batch", [(i, i ^ mask) for i in range(nbatch)])

    *pays, own = pack(cap, owner_rows, offsets, intensities, object_field, fixed[2])
    pays = [pays[0]] + [swap(pays[m], m) for m in range(1, nbatch)]
    other = swap(own, 1)
    padded = extended(object_field, (("batch", 2), ("tile", 3)), 1)
    smoothing = tv_local(padded)
    carried = ()
    for group in (pays[:2], pays[2:-2], pays[-2:]):
        carried = visits(cap, group, own, other, probe_wave, fixed, carried)
    sums, probe_local = carried
    sums = sums.transpose(0, 1, 2, 4, 3, 5).reshape(2, *object_field.shape)
    field_grad = sums[0] + swap(sums[1].astype(bf16), 1).astype(f32)
    probe_total = lax.psum(probe_local, ("batch", "tile"))
    new_object = object_field - update_rate * (field_grad + tv_weight * smoothing)
    new_probe = probe_wave.astype(f32) - probe_rate * probe_total
    return (new_object, new_probe)


def solution(mesh):
    return jax.shard_map(
        on_device,
        mesh=mesh,
        in_specs=(
            P(None, None, "batch", "tile"),
            P(),
            P(("batch", "tile"), None, None),
            P(("batch", "tile"), None),
            P(("batch", "tile"), None),
        ),
        out_specs=(P(None, None, "batch", "tile"), P()),
        check_vma=False,
    )
```

```python
import math

import jax
import jax.numpy as jnp
import ml_dtypes
import numpy as np
from jax import lax
from jax.experimental import pallas as pl
from jax.experimental.pallas import tpu as pltpu
from jax.sharding import PartitionSpec as P

update_rate = 0.1
tv_weight = 12.0
tv_smooth = 1.0
probe_rate = 0.04
lanes = 128
block = 16
fields = 4
tail_rows = 16
f32, bf16 = jnp.float32, jnp.bfloat16


def tables(extent):
    half = extent // 2
    counter = np.arange(extent)
    angles = (counter[:, None] * counter[None, :] % extent) * (2.0 * math.pi / extent)
    scaling = 1.0 / math.sqrt(extent)
    cos_table, sin_table = np.cos(angles) * scaling, -np.sin(angles) * scaling

    def packed(first):
        real, imag = cos_table[first::2, :half], sin_table[first::2, :half]
        return np.block([[real, -imag], [imag, real]])

    even, odd = packed(0), packed(1)
    order = np.concatenate([counter[0::2], counter[1::2]])
    squared = (((order + half) % extent - half) ** 2).astype(np.float64)
    phases = -(0.5 / extent) * (squared[:, None] + squared[None, :])
    sort = counter[:, None] == order[None, :]
    return (
        np.stack([even, odd, even.T, odd.T]).astype(np.float32).astype(ml_dtypes.bfloat16),
        np.stack([np.cos(phases), np.sin(phases)]).astype(np.float32),
        np.stack([sort, sort.T]).astype(ml_dtypes.bfloat16),
    )


def dot(a, b):
    return jnp.dot(a, b, preferred_element_type=f32)


def visit_stages(tile, row_at, col_at, measured, probe, tabs, prop, wide, summed, total, work):
    near, far, mid_near, mid_far, psi, trans = work
    extent = near.shape[-1]
    half = extent // 2
    slices = trans.shape[0]
    even, odd, even_t, odd_t = (tabs.at[i] for i in range(4))
    rest = lax.rem(col_at, lanes)
    base = lax.div(col_at, lanes)
    back = lax.rem(lanes - rest, lanes)
    lane = lax.broadcasted_iota(jnp.int32, (block, lanes), 1)
    keep = lane < lanes - rest
    ahead = lane >= rest
    last = wide.shape[3] - 1
    spots = [jnp.minimum(base + j, last) for j in range(3)]
    halves = (slice(0, half), slice(half, extent))

    def cut(slab, part, r):
        rows = pl.ds(row_at + r, block)
        cols = [pltpu.roll(wide[tile, slab, part, spots[j], rows, :], back, 1) for j in range(3)]
        pair = [jnp.where(keep, cols[j], cols[j + 1]) for j in range(2)]
        for h in range(2):
            trans[slab, part, r:r + block, halves[h]] = pair[h]
        return pair

    def add(slab, part, r, pair):
        left, right = [pltpu.roll(x.astype(bf16).astype(f32), rest, 1) for x in pair]
        rows = pl.ds(row_at + r, block)
        summed[tile, slab, part, spots[0], rows, :] += jnp.where(ahead, left, 0.0)
        summed[tile, slab, part, spots[1], rows, :] += jnp.where(ahead, right, left)
        summed[tile, slab, part, spots[2], rows, :] += jnp.where(ahead, 0.0, right)

    def enter(r, real, imag):
        for k, x in enumerate((real, imag)):
            rows = slice(k * half + r, k * half + r + block)
            for h in range(2):
                near[rows, halves[h]] = (x[0][h] + x[1][h]).astype(bf16)
                far[rows, halves[h]] = (x[0][h] - x[1][h]).astype(bf16)

    def place(r, h, real, imag):
        to = near if r < half else far
        at = r % half
        to[at:at + block, halves[h]] = real.astype(bf16)
        to[half + at:half + at + block, halves[h]] = imag.astype(bf16)

    def outward_left():
        for table, x, at in ((even, near, 0), (odd, far, half)):
            y = dot(table[...], x[...])
            for r in range(0, half, block):
                for k in range(2):
                    rows = slice(k * half + r, k * half + r + block)
                    a, b = y[rows, :half], y[rows, half:]
                    mid_near[at + r:at + r + block, halves[k]] = (a + b).astype(bf16)
                    mid_far[at + r:at + r + block, halves[k]] = (a - b).astype(bf16)

    def outward_right(use):
        for h, (x, table) in enumerate(((mid_near, even_t), (mid_far, odd_t))):
            y = dot(x[...], table[...])
            for r in range(0, extent, block):
                use(r, h, y[r:r + block, :half], y[r:r + block, half:])

    def inward_left():
        e = dot(even_t[...], near[...])
        o = dot(odd_t[...], far[...])
        for r in range(0, half, block):
            for k in range(2):
                rows = slice(k * half + r, k * half + r + block)
                for h, to in enumerate((mid_near, mid_far)):
                    a, b = e[rows, halves[h]], o[rows, halves[h]]
                    to[r:r + block, halves[k]] = (a + b).astype(bf16)
                    to[half + r:half + r + block, halves[k]] = (a - b).astype(bf16)

    def inward_right(use):
        e = dot(mid_near[...], even[...])
        o = dot(mid_far[...], odd[...])
        for r in range(0, half, block):
            real, imag = [], []
            for at in (r, half + r):
                for into, c in ((real, halves[0]), (imag, halves[1])):
                    a, b = e[at:at + block, c], o[at:at + block, c]
                    into.append([a + b, a - b])
            use(r, real, imag)

    groups = lambda r: (r, half + r)

    def times(w, t):
        wr, wi = w
        tr, ti = t
        return wr * tr - wi * ti, wr * ti + wi * tr

    def first(r):
        out = [], []
        for at in groups(r):
            t = [cut(0, part, at) for part in range(2)]
            rows = slice(at, at + block)
            pair = [times([probe[part, rows, halves[h]] for part in range(2)], [t[part][h] for part in range(2)]) for h in range(2)]
            for part in range(2):
                out[part].append([p[part] for p in pair])
        enter(r, *out)

    for r in range(0, half, block):
        first(r)
    yield

    def kick(r, h, fr, fi):
        pr, pi = (prop[part, r:r + block, halves[h]] for part in range(2))
        place(r, h, pr * fr - pi * fi, pr * fi + pi * fr)

    def kick_back(r, h, bi, br):
        pr, pi = (prop[part, r:r + block, halves[h]] for part in range(2))
        place(r, h, pr * bi - pi * br, pr * br + pi * bi)

    def entering(slab):
        def use(r, real, imag):
            out = [], []
            for g, at in enumerate(groups(r)):
                rows = slice(at, at + block)
                t = [cut(slab, part, at) for part in range(2)]
                pair = []
                for h in range(2):
                    w = [x[g][h].astype(bf16).astype(f32) for x in (real, imag)]
                    for part in range(2):
                        psi[slab - 1, part, rows, halves[h]] = w[part]
                    pair.append(times(w, [t[part][h] for part in range(2)]))
                for part in range(2):
                    out[part].append([p[part] for p in pair])
            enter(r, *out)
        return use

    for slab in range(1, slices):
        outward_left()
        yield
        outward_right(kick)
        yield
        inward_left()
        yield
        inward_right(entering(slab))
        yield
    outward_left()
    yield

    def residual(r, h, fr, fi):
        misfit = 0.5 * (fr * fr + fi * fi - measured(r, h))
        place(r, h, misfit * fr, misfit * fi)

    outward_right(residual)
    yield
    inward_left()
    yield

    def leaving(slab, swapped):
        def use(r, real, imag):
            if swapped:
                real, imag = imag, real
            out = [], []
            for g, at in enumerate(groups(r)):
                rows = slice(at, at + block)
                grads, back_ = [], []
                for h in range(2):
                    gr, gi = real[g][h], imag[g][h]
                    if slab == 0:
                        wr, wi = (probe[part, rows, halves[h]] for part in range(2))
                    else:
                        wr, wi = (psi[slab - 1, part, rows, halves[h]] for part in range(2))
                    tr, ti = (trans[slab, part, rows, halves[h]] for part in range(2))
                    grads.append((gr * wr + gi * wi, gi * wr - gr * wi))
                    back_.append((gr * tr + gi * ti, gi * tr - gr * ti))
                for part in range(2):
                    add(slab, part, at, [x[part] for x in grads])
                    if slab == 0:
                        for h in range(2):
                            total[part, rows, halves[h]] += back_[h][part]
                    out[part].append([x[part] for x in back_])
            if slab > 0:
                enter(r, out[1], out[0])
        return use

    inward_right(leaving(slices - 1, False))
    yield
    for slab in range(slices - 1, 0, -1):
        outward_left()
        yield
        outward_right(kick_back)
        yield
        inward_left()
        yield
        inward_right(leaving(slab - 1, True))
        yield

def run_together(stages):
    stages = list(stages)
    live = [True] * len(stages)
    tick = 0
    while any(live):
        for i, s in enumerate(stages):
            if live[i] and tick >= i:
                try:
                    next(s)
                except StopIteration:
                    live[i] = False
        tick += 1


def visits_kernel(cap, first, last, sources, *refs):
    pays = refs[:sources]
    own_ref, other_ref, probe_ref, tables_ref, prop_ref = refs[sources : sources + 5]
    carried = refs[sources + 5 : sources + 5 + (0 if first else 2)]
    rest = refs[sources + 5 + len(carried) :]
    if last:
        sums_out, other_out, total_ref, *rest, sums_ref = rest
    else:
        sums_ref, total_ref, *rest = rest
    wide, held, probe, notes, plan, listed, pay_sem, sem, *work = rest
    extent = probe_ref.shape[-1]
    copies = [
        pltpu.make_async_copy(pay, held.at[s], pay_sem.at[s]) for s, pay in enumerate(pays)
    ]
    for copy in copies:
        copy.start()
    for t, tile_ref in enumerate((own_ref, other_ref)):
        wide[t] = tile_ref[...].astype(f32)
    probe[...] = probe_ref[...].astype(f32)
    if first:
        sums_ref[...] = jnp.zeros_like(sums_ref)
        total_ref[...] = jnp.zeros_like(total_ref)
    else:
        sums_ref[...] = carried[0][...]
        total_ref[...] = carried[1][...]
    for copy in copies:
        copy.wait()
    for s in range(sources):
        tail = held[s, cap * extent : cap * extent + tail_rows, :lanes]
        notes[s * 8 : s * 8 + 8] = tail.astype(f32)[:8].astype(jnp.int32)
    copy = pltpu.make_async_copy(notes, plan, sem)
    copy.start()
    copy.wait()
    count = jnp.int32(0)
    for s in range(sources):
        for i in range(cap):
            listed[count] = s * cap + i
            count = count + plan[s * 8, i * fields]

    def one(k, lane):
        at = listed[k]
        source, slot = lax.div(at, cap), lax.rem(at, cap)
        tile, row_at, col_at = (plan[source * 8, slot * fields + j] for j in (1, 2, 3))

        def measured(r, h):
            rows = pl.ds(pl.multiple_of(slot * extent + r, block), block)
            return held[source, rows, h * lanes : (h + 1) * lanes].astype(f32)

        return visit_stages(
            tile, row_at, col_at, measured, probe, tables_ref, prop_ref,
            wide, sums_ref, total_ref, [w.at[lane] for w in work],
        )

    def pair(i, carry):
        run_together([one(2 * i, 0), one(2 * i + 1, 1)])
        return carry

    lax.fori_loop(0, lax.div(count, 2), pair, 0)

    @pl.when(lax.rem(count, 2) == 1)
    def _():
        run_together([one(count - 1, 0)])

    if last:
        sums_out[...] = sums_ref[0]
        other_out[...] = sums_ref[1].astype(bf16)


def visits(cap, pays, own, other, probe, fixed, carried, last):
    tabs, prop, _ = fixed
    slices = own.shape[0]
    extent = probe.shape[-1]
    sources = len(pays)
    shape = (2, *own.shape)
    vmem = pl.BlockSpec(memory_space=pltpu.VMEM)

    def kernel(*refs):
        visits_kernel(cap, not carried, last, sources, *refs)

    operands = (*pays, own, other, probe, tabs, prop, *carried)
    return pl.pallas_call(
        kernel,
        in_specs=[pl.BlockSpec(memory_space=pl.ANY)] * sources
        + [vmem] * (len(operands) - sources),
        out_specs=[vmem] * (3 if last else 2),
        out_shape=(
            [jax.ShapeDtypeStruct(shape[1:], f32), jax.ShapeDtypeStruct(shape[1:], bf16)]
            if last
            else [jax.ShapeDtypeStruct(shape, f32)]
        )
        + [jax.ShapeDtypeStruct((2, extent, extent), f32)],
        scratch_shapes=[
            pltpu.VMEM(shape, f32),
            pltpu.VMEM((sources, *pays[0].shape), bf16),
            pltpu.VMEM(probe.shape, f32),
            pltpu.VMEM((8 * sources, lanes), jnp.int32),
            pltpu.SMEM((8 * sources, lanes), jnp.int32),
            pltpu.SMEM((sources * cap + 1,), jnp.int32),
            pltpu.SemaphoreType.DMA((sources,)),
            pltpu.SemaphoreType.DMA,
        ]
        + [pltpu.VMEM((2, extent, extent), bf16)] * 4
        + [
            pltpu.VMEM((2, slices - 1, 2, extent, extent), f32),
            pltpu.VMEM((2, slices, 2, extent, extent), f32),
        ]
        + [pltpu.VMEM(shape, f32)] * last,
        compiler_params=pltpu.CompilerParams(vmem_limit_bytes=36 * 1024 * 1024),
        cost_estimate=pl.CostEstimate(
            flops=sources * cap * 3 * slices * 16 * extent**3,
            bytes_accessed=16 * 1024 * 1024,
            transcendentals=0,
        ),
    )(*operands)


def pack_kernel(cap, nbatch, owner_ref, offset_ref, measured_ref, sort_ref, *refs):
    outs = refs[:nbatch]
    index, count, held, ready, tails, in_sem, out_sem, tail_sem = refs[nbatch:]
    positions, extent = measured_ref.shape[0], measured_ref.shape[-1]
    me = lax.axis_index("batch")

    def load(p):
        return pltpu.make_async_copy(measured_ref.at[p], held.at[p], in_sem.at[p])

    for p in range(positions):
        load(p).start()

    def clear(i, carry):
        index[i] = -1
        return carry

    lax.fori_loop(0, nbatch * cap, clear, 0)

    def clear_count(i, carry):
        count[i] = 0
        return carry

    lax.fori_loop(0, nbatch, clear_count, 0)

    def place(p, carry):
        row = owner_ref[p]
        rank = count[row]
        count[row] = rank + 1
        bit = lax.rem(row, 2)
        dest = row - bit + lax.rem(rank + row + me, 2)
        slot = bit * (cap // 2) + lax.div(rank, 2)
        index[jnp.bitwise_xor(dest, me) * cap + slot] = p
        return carry

    lax.fori_loop(0, positions, place, 0)
    lane = lax.broadcasted_iota(jnp.int32, (tail_rows, extent), 1)
    tail_copies = []
    for mask in range(nbatch):
        dest_bit = lax.rem(jnp.bitwise_xor(me, mask), 2)
        tail = jnp.zeros((tail_rows, extent), jnp.int32)
        for slot in range(cap):
            p = index[mask * cap + slot]
            at = jnp.maximum(p, 0)
            note = (
                jnp.where(p >= 0, 1, 0),
                jnp.where(dest_bit == slot // (cap // 2), 0, 1),
                offset_ref[2 * at],
                offset_ref[2 * at + 1],
            )
            for k, value in enumerate(note):
                tail = jnp.where(lane == slot * fields + k, value, tail)
        tails[mask] = tail.astype(f32).astype(bf16)
        copy = pltpu.make_async_copy(
            tails.at[mask], outs[mask].at[pl.ds(cap * extent, tail_rows)], tail_sem.at[mask]
        )
        copy.start()
        tail_copies.append(copy)
    for p in range(positions):
        load(p).wait()
        across = dot(held[p].astype(bf16), sort_ref[0]).astype(bf16)
        ready[p] = dot(sort_ref[1], across).astype(bf16)

    def store(mask, slot, p):
        k = mask * cap + slot
        return pltpu.make_async_copy(
            ready.at[p], outs[mask].at[pl.ds(slot * extent, extent)], out_sem.at[k]
        )

    for act in ("start", "wait"):
        for mask in range(nbatch):
            for slot in range(cap):
                p = index[mask * cap + slot]

                @pl.when(p >= 0)
                def _(mask=mask, slot=slot, p=p, act=act):
                    getattr(store(mask, slot, p), act)()

    for copy in tail_copies:
        copy.wait()


def pack(cap, owner_rows, offsets, intensities, sort):
    nbatch = lax.axis_size("batch")
    positions, extent = intensities.shape[0], intensities.shape[-1]
    smem = pl.BlockSpec(memory_space=pltpu.SMEM)
    vmem = pl.BlockSpec(memory_space=pltpu.VMEM)
    anywhere = pl.BlockSpec(memory_space=pl.ANY)

    def kernel(*refs):
        pack_kernel(cap, nbatch, *refs)

    return pl.pallas_call(
        kernel,
        in_specs=[smem, smem, anywhere, vmem],
        out_specs=[anywhere] * nbatch,
        out_shape=[jax.ShapeDtypeStruct((cap * extent + tail_rows, extent), bf16)] * nbatch,
        scratch_shapes=[
            pltpu.SMEM((nbatch * cap,), jnp.int32),
            pltpu.SMEM((nbatch,), jnp.int32),
            pltpu.VMEM(intensities.shape, f32),
            pltpu.VMEM(intensities.shape, bf16),
            pltpu.VMEM((nbatch, tail_rows, extent), bf16),
            pltpu.SemaphoreType.DMA((positions,)),
            pltpu.SemaphoreType.DMA((nbatch * cap,)),
            pltpu.SemaphoreType.DMA((nbatch,)),
        ],
        compiler_params=pltpu.CompilerParams(vmem_limit_bytes=60 * 1024 * 1024),
    )(owner_rows.reshape(-1), offsets.reshape(-1), intensities, sort)


def sender(send_sem, recv_sem):
    def send(source, target, device, *index):
        copy = pltpu.make_async_remote_copy(
            src_ref=source, dst_ref=target,
            send_sem=send_sem.at[index] if index else send_sem,
            recv_sem=recv_sem.at[index] if index else recv_sem,
            device_id=device, device_id_type=pl.DeviceIdType.MESH,
        )
        copy.start()
        return copy

    return send


def places():
    nbatch, ntile = lax.axis_size("batch"), lax.axis_size("tile")
    at, col = lax.axis_index("batch"), lax.axis_index("tile")

    def along_batch(r):
        return (lax.rem(at + r, nbatch), col)

    def along_tile(r):
        return (at, lax.rem(col + r, ntile))

    return nbatch, ntile, at, col, along_batch, along_tile


def greet():
    nbatch, ntile, _, _, along_batch, along_tile = places()
    barrier = pltpu.get_barrier_semaphore()
    mesh_id = pl.DeviceIdType.MESH
    for r in range(1, nbatch):
        pl.semaphore_signal(barrier, inc=1, device_id=along_batch(r), device_id_type=mesh_id)
    for r in range(1, ntile):
        pl.semaphore_signal(barrier, inc=1, device_id=along_tile(r), device_id_type=mesh_id)
    return lambda: pl.semaphore_wait(barrier, nbatch - 1 + ntile - 1)


def border_kernel(
    field_ref, pay_ref, base_ref, own_ref, other_ref, got_ref,
    pad, falls, rest, edge, beside, row_out, row_in,
    load_sem, pay_sem, tile_sem, edge_sem, row_sem,
):
    nbatch, ntile, at, col, along_batch, along_tile = places()
    slices, _, height, width = field_ref.shape
    planes = 2 * slices
    loads = []
    for q in range(planes):
        load = pltpu.make_async_copy(
            field_ref.at[q // 2, q % 2], pad.at[q, pl.ds(8, height), :], load_sem.at[q]
        )
        load.start()
        loads.append(load)
    everyone_in = greet()
    for load in loads:
        load.wait()
    lane = lax.broadcasted_iota(jnp.int32, (height, lanes), 1)
    edges = jnp.zeros((height, lanes), f32)
    for q in range(planes):
        edges = jnp.where(lane == q, pad[q, 8 : 8 + height, width - 1 : width], edges)
        edges = jnp.where(lane == planes + q, pad[q, 8 : 8 + height, 0:1], edges)
    edge[...] = edges
    everyone_in()
    send = sender(edge_sem.at[0], edge_sem.at[1])
    sides = [
        send(edge, beside.at[0], along_tile(1), 0),
        send(edge, beside.at[1], along_tile(ntile - 1), 1),
    ]
    sibling = (at + 1 - 2 * lax.rem(at, 2), col)
    pay_sent = sender(pay_sem.at[0], pay_sem.at[1])(pay_ref, got_ref, sibling)
    for q in range(planes):
        for j in range(width // lanes):
            cols = slice(j * lanes, (j + 1) * lanes)
            own_ref[q // 2, q % 2, j] = pad[q, 8 : 8 + height, cols].astype(bf16)
    tile_sent = sender(tile_sem.at[0], tile_sem.at[1])(own_ref, other_ref, sibling)
    for copy in sides:
        copy.wait()
    for q in range(planes):
        first = beside[0, 0:1, q : q + 1]
        last = beside[1, height - 1 : height, planes + q : planes + q + 1]
        row_out[0, q : q + 1, :width] = pad[q, 8:9, :]
        row_out[0, q : q + 1, width:] = jnp.broadcast_to(first, (1, lanes))
        row_out[1, q : q + 1, :width] = pad[q, 7 + height : 8 + height, :]
        row_out[1, q : q + 1, width:] = jnp.broadcast_to(last, (1, lanes))
    send = sender(row_sem.at[0], row_sem.at[1])
    ends = [
        send(row_out.at[0], row_in.at[0], along_batch(nbatch - 1), 0),
        send(row_out.at[1], row_in.at[1], along_batch(1), 1),
    ]
    for copy in ends:
        copy.wait()
    for q in range(planes):
        pad[q, 7:8, :] = row_in[1, q : q + 1, :width]
        pad[q, 8 + height : 9 + height, :] = row_in[0, q : q + 1, :width]

    def weighed(downs, rights):
        squares = sum(d * d for d in downs) + sum(d * d for d in rights)
        return lax.rsqrt(squares + tv_smooth)

    def flows(block):
        place = lax.broadcasted_iota(jnp.int32, (block, width), 1)
        for slab in range(slices):
            pair = (2 * slab, 2 * slab + 1)
            above = [pad[q, 7:8, :] for q in pair]
            corner = [row_in[1, q : q + 1, width : width + 1] for q in pair]
            downs = [pad[q, 8:9, :] - x for q, x in zip(pair, above)]
            rights = [
                jnp.where(place[:1] == width - 1, c, pltpu.roll(x, width - 1, 1)) - x
                for c, x in zip(corner, above)
            ]
            weight = weighed(downs, rights)
            for q, d in zip(pair, downs):
                falls[q, 7:8, :] = weight * d
            for start in range(0, height, block):
                here = [pad[q, 8 + start : 8 + start + block, :] for q in pair]
                below = [pad[q, 9 + start : 9 + start + block, :] for q in pair]
                edge_right = [
                    beside[1, start : start + block, planes + q : planes + q + 1] for q in pair
                ]
                downs = [b - x for b, x in zip(below, here)]
                rights = [
                    jnp.where(place == width - 1, e, pltpu.roll(x, width - 1, 1)) - x
                    for e, x in zip(edge_right, here)
                ]
                weight = weighed(downs, rights)
                left = [beside[0, start : start + block, q : q + 1] for q in pair]
                if start + block < height:
                    left_down = [beside[0, start + 1 : start + block + 1, q : q + 1] for q in pair]
                else:
                    left_down = [
                        jnp.concatenate(
                            [
                                beside[0, start + 1 : height, q : q + 1],
                                row_in[0, q : q + 1, width : width + 1],
                            ],
                            0,
                        )
                        for q in pair
                    ]
                left_rights = [x[:, :1] - l for x, l in zip(here, left)]
                left_weight = weighed([b - l for b, l in zip(left_down, left)], left_rights)
                for q, d, e, g in zip(pair, downs, rights, left_rights):
                    fall, run = weight * d, weight * e
                    before = jnp.where(place == 0, left_weight * g, pltpu.roll(run, 1, 1))
                    falls[q, 8 + start : 8 + start + block, :] = fall
                    rest[q, start : start + block, :] = before - run - fall

    flows(32)
    for q in range(planes):
        for j in range(width // lanes):
            cols = slice(j * lanes, (j + 1) * lanes)
            tv = falls[q, 7 : 7 + height, cols] + rest[q, :, cols]
            here = pad[q, 8 : 8 + height, cols]
            base_ref[q // 2, q % 2, :, cols] = here - update_rate * tv_weight * tv
    tile_sent.wait()
    pay_sent.wait()


def border(field, pay):
    slices, _, height, width = field.shape
    planes = 2 * slices
    vmem = pl.BlockSpec(memory_space=pltpu.VMEM)
    anywhere = pl.BlockSpec(memory_space=pl.ANY)
    dma = pltpu.SemaphoreType.DMA
    tile = jax.ShapeDtypeStruct((slices, 2, width // lanes, height, lanes), bf16)
    return pl.pallas_call(
        border_kernel,
        in_specs=[anywhere, anywhere],
        out_specs=(vmem, vmem, vmem, anywhere),
        out_shape=(
            jax.ShapeDtypeStruct(field.shape, f32),
            tile,
            tile,
            jax.ShapeDtypeStruct(pay.shape, bf16),
        ),
        scratch_shapes=[
            pltpu.VMEM((planes, height + 16, width), f32),
            pltpu.VMEM((planes, height + 8, width), f32),
            pltpu.VMEM((planes, height, width), f32),
            pltpu.VMEM((height, lanes), f32),
            pltpu.VMEM((2, height, lanes), f32),
            pltpu.VMEM((2, 8, width + lanes), f32),
            pltpu.VMEM((2, 8, width + lanes), f32),
            dma((planes,)),
            dma((2,)),
            dma((2,)),
            dma((2, 2)),
            dma((2, 2)),
        ],
        compiler_params=pltpu.CompilerParams(
            vmem_limit_bytes=40 * 1024 * 1024, collective_id=1, has_side_effects=True
        ),
        cost_estimate=pl.CostEstimate(
            flops=60 * field.size, bytes_accessed=16 * field.size, transcendentals=field.size
        ),
    )(field, pay)


def finish_kernel(
    sums_ref, other_ref, total_ref, probe_ref, grad_ref, new_probe_ref,
    taken, mine, gathered, share, whole, sum_sem, gather_sem, share_sem, spread_sem,
):
    nbatch, ntile, at, col, along_batch, along_tile = places()
    extent = probe_ref.shape[-1]
    chunk = 2 * extent // nbatch
    everyone_in = greet()
    for part in range(2):
        mine[part * extent : (part + 1) * extent] = total_ref[part].astype(bf16)
    everyone_in()
    send = sender(gather_sem.at[0], gather_sem.at[1])
    gathers = []
    for r in range(1, nbatch):
        rows = pl.ds(lax.rem(at + r, nbatch) * chunk, chunk)
        gathers.append(send(mine.at[rows], gathered.at[r - 1], along_batch(r), r - 1))
    sibling = (at + 1 - 2 * lax.rem(at, 2), col)
    summed = sender(sum_sem.at[0], sum_sem.at[1])(other_ref, taken, sibling)
    for copy in gathers:
        copy.wait()
    part = mine[pl.ds(at * chunk, chunk)].astype(f32)
    for r in range(1, nbatch):
        part = part + gathered[r - 1].astype(f32)
    share[pl.ds(col, 1)] = part.astype(bf16)[None]
    send = sender(share_sem.at[0], share_sem.at[1])
    shares = [
        send(share.at[col], share.at[col], along_tile(r), r - 1) for r in range(1, ntile)
    ]
    summed.wait()
    slices, _, cols, _, _ = sums_ref.shape
    for slab in range(slices):
        for p in range(2):
            for j in range(cols):
                total = sums_ref[slab, p, j] + taken[slab, p, j].astype(f32)
                grad_ref[slab, p, :, j * lanes : (j + 1) * lanes] = total
    for copy in shares:
        copy.wait()
    final = share[0].astype(f32)
    for i in range(1, ntile):
        final = final + share[i].astype(f32)
    own_rows = pl.ds(at * chunk, chunk)
    whole[own_rows] = final.astype(bf16)
    send = sender(spread_sem.at[0], spread_sem.at[1])
    spreads = [
        send(whole.at[own_rows], whole.at[own_rows], along_batch(r), r - 1)
        for r in range(1, nbatch)
    ]
    for copy in spreads:
        copy.wait()
    for part in range(2):
        rows = slice(part * extent, (part + 1) * extent)
        new_probe_ref[part] = probe_ref[part].astype(f32) - probe_rate * whole[rows].astype(f32)


def finish(sums, other, total, probe, shape):
    nbatch, ntile = lax.axis_size("batch"), lax.axis_size("tile")
    extent = probe.shape[-1]
    chunk = 2 * extent // nbatch
    vmem = pl.BlockSpec(memory_space=pltpu.VMEM)
    dma = pltpu.SemaphoreType.DMA
    return pl.pallas_call(
        finish_kernel,
        in_specs=[vmem] * 4,
        out_specs=(vmem, vmem),
        out_shape=(
            jax.ShapeDtypeStruct(shape, f32),
            jax.ShapeDtypeStruct(probe.shape, f32),
        ),
        scratch_shapes=[
            pltpu.VMEM(other.shape, bf16),
            pltpu.VMEM((2 * extent, extent), bf16),
            pltpu.VMEM((nbatch - 1, chunk, extent), bf16),
            pltpu.VMEM((ntile, chunk, extent), bf16),
            pltpu.VMEM((2 * extent, extent), bf16),
            dma((2,)),
            dma((2, nbatch - 1)),
            dma((2, ntile - 1)),
            dma((2, nbatch - 1)),
        ],
        compiler_params=pltpu.CompilerParams(
            vmem_limit_bytes=20 * 1024 * 1024, collective_id=0, has_side_effects=True
        ),
        cost_estimate=pl.CostEstimate(
            flops=4 * sums.size, bytes_accessed=16 * sums.size, transcendentals=0
        ),
    )(sums, other, total, probe)


def on_device(object_field, probe_wave, intensities, owner_rows, offsets):
    extent = probe_wave.shape[-1]
    nbatch = lax.axis_size("batch")
    cap = max(2, 2 * intensities.shape[0] // nbatch)
    fixed = tuple(jnp.asarray(x) for x in tables(extent))

    def swap(x, mask):
        return lax.ppermute(x, "batch", [(i, i ^ mask) for i in range(nbatch)])

    pays = pack(cap, owner_rows, offsets, intensities, fixed[2])
    field, *pays = lax.optimization_barrier((object_field, *pays))
    base, own, other, got = border(field, pays[1])
    pays = [pays[0], got] + [swap(pays[m], m) for m in range(2, nbatch)]
    groups = (pays[:2], pays[2:-2], pays[-2:])
    carried = ()
    for i, group in enumerate(groups):
        carried = visits(
            cap, group, own, other, probe_wave, fixed, carried, i + 1 == len(groups)
        )
    sums, returned, total = carried
    grad, new_probe = finish(sums, returned, total, probe_wave, object_field.shape)
    return (base - update_rate * grad, new_probe)


def solution(mesh):
    return jax.shard_map(
        on_device,
        mesh=mesh,
        in_specs=(
            P(None, None, "batch", "tile"),
            P(),
            P(("batch", "tile"), None, None),
            P(("batch", "tile"), None),
            P(("batch", "tile"), None),
        ),
        out_specs=(P(None, None, "batch", "tile"), P()),
        check_vma=False,
    )
```

```python
import math

import jax
import jax.numpy as jnp
import ml_dtypes
import numpy as np
from jax import lax
from jax.experimental import pallas as pl
from jax.experimental.pallas import tpu as pltpu
from jax.sharding import PartitionSpec as P

update_rate = 0.1
tv_weight = 12.0
tv_smooth = 1.0
probe_rate = 0.04
lanes = 128
block = 32
together_at_once = 3
fields = 4
tail_rows = 16
f32, bf16 = jnp.float32, jnp.bfloat16


def tables(extent):
    half = extent // 2
    counter = np.arange(extent)
    angles = (counter[:, None] * counter[None, :] % extent) * (2.0 * math.pi / extent)
    scaling = 1.0 / math.sqrt(extent)
    cos_table, sin_table = np.cos(angles) * scaling, -np.sin(angles) * scaling

    def packed(first):
        real, imag = cos_table[first::2, :half], sin_table[first::2, :half]
        return np.block([[real, -imag], [imag, real]])

    even, odd = packed(0), packed(1)
    order = np.concatenate([counter[0::2], counter[1::2]])
    squared = ((counter + half) % extent - half).astype(np.float64) ** 2
    phases = -(0.5 / extent) * (squared[:, None] + squared[order][None, :])
    sort = counter[:, None] == order[None, :]

    def whole(sine):
        return np.block([[cos_table, -sine], [sine, cos_table]])

    def as_bf16(x):
        return jnp.asarray(np.asarray(x).astype(np.float32).astype(ml_dtypes.bfloat16))

    return (
        (
            as_bf16(np.stack([whole(sin_table), whole(-sin_table)])),
            as_bf16(np.stack([even, odd, even.T, odd.T])),
        ),
        jnp.asarray(np.stack([np.cos(phases), np.sin(phases)]).astype(np.float32)),
        as_bf16(sort),
    )


def dot(a, b):
    return jnp.dot(a, b, preferred_element_type=f32)


def visit_stages(tile, row_at, col_at, measured, probe, tabs, prop, wide, summed, total, work):
    field, mid_near, mid_far, psi, trans = work
    left, tabs = tabs
    extent = field.shape[-1]
    half = extent // 2
    slices = trans.shape[0]
    even, odd, even_t, odd_t = (tabs.at[i] for i in range(4))
    rest = lax.rem(col_at, lanes)
    base = lax.div(col_at, lanes)
    back = lax.rem(lanes - rest, lanes)
    lane = lax.broadcasted_iota(jnp.int32, (block, lanes), 1)
    keep = lane < lanes - rest
    ahead = lane >= rest
    last = wide.shape[3] - 1
    spots = [jnp.minimum(base + j, last) for j in range(3)]
    halves = (slice(0, half), slice(half, extent))

    def cut(slab, part, r):
        rows = pl.ds(row_at + r, block)
        cols = [pltpu.roll(wide[tile, slab, part, spots[j], rows, :], back, 1) for j in range(3)]
        pair = [jnp.where(keep, cols[j], cols[j + 1]) for j in range(2)]
        for h in range(2):
            trans[slab, part, r:r + block, halves[h]] = pair[h]
        return pair

    def add(slab, part, r, pair):
        left, right = [pltpu.roll(x.astype(bf16).astype(f32), rest, 1) for x in pair]
        rows = pl.ds(row_at + r, block)
        summed[tile, slab, part, spots[0], rows, :] += jnp.where(ahead, left, 0.0)
        summed[tile, slab, part, spots[1], rows, :] += jnp.where(ahead, right, left)
        summed[tile, slab, part, spots[2], rows, :] += jnp.where(ahead, 0.0, right)

    def enter(r, real, imag):
        for k, x in enumerate((real, imag)):
            for g, at in enumerate((r, half + r)):
                rows = slice(k * extent + at, k * extent + at + block)
                for h in range(2):
                    field[rows, halves[h]] = x[g][h].astype(bf16)

    def place(r, h, real, imag):
        field[r : r + block, halves[h]] = real.astype(bf16)
        field[extent + r : extent + r + block, halves[h]] = imag.astype(bf16)

    def outward_left():
        for k in range(2):
            y = dot(left[0, k * extent : (k + 1) * extent], field[...])
            for r in range(0, extent, block):
                a, b = y[r : r + block, :half], y[r : r + block, half:]
                mid_near[r : r + block, halves[k]] = (a + b).astype(bf16)
                mid_far[r : r + block, halves[k]] = (a - b).astype(bf16)

    def outward_right(use):
        for h, (x, table) in enumerate(((mid_near, even_t), (mid_far, odd_t))):
            y = dot(x[...], table[...])
            for r in range(0, extent, block):
                use(r, h, y[r:r + block, :half], y[r:r + block, half:])

    def inward_left():
        for k in range(2):
            y = dot(left[1, k * extent : (k + 1) * extent], field[...])
            for r in range(0, extent, block):
                for h, to in enumerate((mid_near, mid_far)):
                    to[r : r + block, halves[k]] = y[r : r + block, halves[h]].astype(bf16)

    def inward_right(use):
        e = dot(mid_near[...], even[...])
        o = dot(mid_far[...], odd[...])
        for r in range(0, half, block):
            real, imag = [], []
            for at in (r, half + r):
                for into, c in ((real, halves[0]), (imag, halves[1])):
                    a, b = e[at:at + block, c], o[at:at + block, c]
                    into.append([a + b, a - b])
            use(r, real, imag)

    groups = lambda r: (r, half + r)

    def times(w, t):
        wr, wi = w
        tr, ti = t
        return wr * tr - wi * ti, wr * ti + wi * tr

    def first(r):
        out = [], []
        for at in groups(r):
            t = [cut(0, part, at) for part in range(2)]
            rows = slice(at, at + block)
            pair = [times([probe[part, rows, halves[h]] for part in range(2)], [t[part][h] for part in range(2)]) for h in range(2)]
            for part in range(2):
                out[part].append([p[part] for p in pair])
        enter(r, *out)

    for r in range(0, half, block):
        first(r)
    yield

    def kick(r, h, fr, fi):
        pr, pi = (prop[part, r:r + block, halves[h]] for part in range(2))
        place(r, h, pr * fr - pi * fi, pr * fi + pi * fr)

    def kick_back(r, h, bi, br):
        pr, pi = (prop[part, r:r + block, halves[h]] for part in range(2))
        place(r, h, pr * bi - pi * br, pr * br + pi * bi)

    def entering(slab):
        def use(r, real, imag):
            out = [], []
            for g, at in enumerate(groups(r)):
                rows = slice(at, at + block)
                t = [cut(slab, part, at) for part in range(2)]
                pair = []
                for h in range(2):
                    w = [x[g][h].astype(bf16).astype(f32) for x in (real, imag)]
                    for part in range(2):
                        psi[slab - 1, part, rows, halves[h]] = w[part]
                    pair.append(times(w, [t[part][h] for part in range(2)]))
                for part in range(2):
                    out[part].append([p[part] for p in pair])
            enter(r, *out)
        return use

    for slab in range(1, slices):
        outward_left()
        yield
        outward_right(kick)
        yield
        inward_left()
        yield
        inward_right(entering(slab))
        yield
    outward_left()
    yield

    def residual(r, h, fr, fi):
        misfit = 0.5 * (fr * fr + fi * fi - measured(r, h))
        place(r, h, misfit * fr, misfit * fi)

    outward_right(residual)
    yield
    inward_left()
    yield

    def leaving(slab, swapped):
        def use(r, real, imag):
            if swapped:
                real, imag = imag, real
            out = [], []
            for g, at in enumerate(groups(r)):
                rows = slice(at, at + block)
                grads, back_ = [], []
                for h in range(2):
                    gr, gi = real[g][h], imag[g][h]
                    if slab == 0:
                        wr, wi = (probe[part, rows, halves[h]] for part in range(2))
                    else:
                        wr, wi = (psi[slab - 1, part, rows, halves[h]] for part in range(2))
                    tr, ti = (trans[slab, part, rows, halves[h]] for part in range(2))
                    grads.append((gr * wr + gi * wi, gi * wr - gr * wi))
                    back_.append((gr * tr + gi * ti, gi * tr - gr * ti))
                for part in range(2):
                    add(slab, part, at, [x[part] for x in grads])
                    if slab == 0:
                        for h in range(2):
                            total[part, rows, halves[h]] += back_[h][part]
                    out[part].append([x[part] for x in back_])
            if slab > 0:
                enter(r, out[1], out[0])
        return use

    inward_right(leaving(slices - 1, False))
    yield
    for slab in range(slices - 1, 0, -1):
        outward_left()
        yield
        outward_right(kick_back)
        yield
        inward_left()
        yield
        inward_right(leaving(slab - 1, True))
        yield

def run_together(stages):
    stages = list(stages)
    live = [True] * len(stages)
    tick = 0
    while any(live):
        for i, s in enumerate(stages):
            if live[i] and tick >= i:
                try:
                    next(s)
                except StopIteration:
                    live[i] = False
        tick += 1


def visits_kernel(cap, first, last, sources, *refs):
    pays = refs[:sources]
    own_ref, other_ref, probe_ref, left_ref, tables_ref, prop_ref = refs[sources : sources + 6]
    carried = refs[sources + 6 : sources + 6 + (0 if first else 2)]
    rest = refs[sources + 6 + len(carried) :]
    if last:
        sums_out, other_out, total_ref, *rest, sums_ref = rest
    else:
        sums_ref, total_ref, *rest = rest
    wide, held, probe, notes, plan, listed, pay_sem, sem, *work = rest
    extent = probe_ref.shape[-1]
    copies = [
        pltpu.make_async_copy(pay, held.at[s], pay_sem.at[s]) for s, pay in enumerate(pays)
    ]
    for copy in copies:
        copy.start()
    for t, tile_ref in enumerate((own_ref, other_ref)):
        wide[t] = tile_ref[...].astype(f32)
    probe[...] = probe_ref[...].astype(f32)
    if first:
        sums_ref[...] = jnp.zeros_like(sums_ref)
        total_ref[...] = jnp.zeros_like(total_ref)
    else:
        sums_ref[...] = carried[0][...]
        total_ref[...] = carried[1][...]
    for copy in copies:
        copy.wait()
    for s in range(sources):
        tail = held[s, cap * extent : cap * extent + tail_rows, :lanes]
        notes[s * 8 : s * 8 + 8] = tail.astype(f32)[:8].astype(jnp.int32)
    copy = pltpu.make_async_copy(notes, plan, sem)
    copy.start()
    copy.wait()
    count = jnp.int32(0)
    for s in range(sources):
        for i in range(cap):
            listed[count] = s * cap + i
            count = count + plan[s * 8, i * fields]

    def one(k, lane):
        at = listed[k]
        source, slot = lax.div(at, cap), lax.rem(at, cap)
        tile, row_at, col_at = (plan[source * 8, slot * fields + j] for j in (1, 2, 3))

        def measured(r, h):
            rows = pl.ds(pl.multiple_of(slot * extent + r, block), block)
            return held[source, rows, h * lanes : (h + 1) * lanes].astype(f32)

        return visit_stages(
            tile, row_at, col_at, measured, probe, (left_ref, tables_ref), prop_ref,
            wide, sums_ref, total_ref, [w.at[lane] for w in work],
        )

    def together(i, carry):
        run_together([one(together_at_once * i + k, k) for k in range(together_at_once)])
        return carry

    def alone(k, carry):
        run_together([one(k, 0)])
        return carry

    groups = lax.div(count, together_at_once)
    lax.fori_loop(0, groups, together, 0)
    lax.fori_loop(groups * together_at_once, count, alone, 0)
    if last:
        sums_out[...] = sums_ref[0]
        other_out[...] = sums_ref[1].astype(bf16)


def visits(cap, pays, own, other, probe, fixed, carried, last):
    (left, right), prop = fixed
    slices = own.shape[0]
    extent = probe.shape[-1]
    sources = len(pays)
    shape = (2, *own.shape)
    vmem = pl.BlockSpec(memory_space=pltpu.VMEM)

    def kernel(*refs):
        visits_kernel(cap, not carried, last, sources, *refs)

    operands = (*pays, own, other, probe, left, right, prop, *carried)
    return pl.pallas_call(
        kernel,
        in_specs=[pl.BlockSpec(memory_space=pl.ANY)] * sources
        + [vmem] * (len(operands) - sources),
        out_specs=[vmem] * (3 if last else 2),
        out_shape=(
            [jax.ShapeDtypeStruct(shape[1:], f32), jax.ShapeDtypeStruct(shape[1:], bf16)]
            if last
            else [jax.ShapeDtypeStruct(shape, f32)]
        )
        + [jax.ShapeDtypeStruct((2, extent, extent), f32)],
        scratch_shapes=[
            pltpu.VMEM(shape, f32),
            pltpu.VMEM((sources, *pays[0].shape), bf16),
            pltpu.VMEM(probe.shape, f32),
            pltpu.VMEM((8 * sources, lanes), jnp.int32),
            pltpu.SMEM((8 * sources, lanes), jnp.int32),
            pltpu.SMEM((sources * cap + 1,), jnp.int32),
            pltpu.SemaphoreType.DMA((sources,)),
            pltpu.SemaphoreType.DMA,
        ]
        + [pltpu.VMEM((together_at_once, 2 * extent, extent), bf16)]
        + [pltpu.VMEM((together_at_once, extent, extent), bf16)] * 2
        + [
            pltpu.VMEM((together_at_once, slices - 1, 2, extent, extent), f32),
            pltpu.VMEM((together_at_once, slices, 2, extent, extent), f32),
        ]
        + [pltpu.VMEM(shape, f32)] * last,
        compiler_params=pltpu.CompilerParams(vmem_limit_bytes=26 * 1024 * 1024),
        cost_estimate=pl.CostEstimate(
            flops=sources * cap * 3 * slices * 16 * extent**3,
            bytes_accessed=16 * 1024 * 1024,
            transcendentals=0,
        ),
    )(*operands)


def plan_kernel(cap, nbatch, owner_ref, offset_ref, index, tails, count):
    extent = tails.shape[-1]
    me = lax.axis_index("batch")

    def clear(i, carry):
        index[i] = -1
        return carry

    lax.fori_loop(0, nbatch * cap, clear, 0)

    def clear_count(i, carry):
        count[i] = 0
        return carry

    lax.fori_loop(0, nbatch, clear_count, 0)

    def place(p, carry):
        row = owner_ref[p]
        rank = count[row]
        count[row] = rank + 1
        bit = lax.rem(row, 2)
        dest = row - bit + lax.rem(rank + row + me, 2)
        slot = bit * (cap // 2) + lax.div(rank, 2)
        index[jnp.bitwise_xor(dest, me) * cap + slot] = p
        return carry

    lax.fori_loop(0, owner_ref.shape[0], place, 0)
    lane = lax.broadcasted_iota(jnp.int32, (tail_rows, extent), 1)
    for mask in range(nbatch):
        dest_bit = lax.rem(jnp.bitwise_xor(me, mask), 2)
        tail = jnp.zeros((tail_rows, extent), jnp.int32)
        for slot in range(cap):
            p = index[mask * cap + slot]
            at = jnp.maximum(p, 0)
            index[mask * cap + slot] = at
            note = (
                jnp.where(p >= 0, 1, 0),
                jnp.where(dest_bit == slot // (cap // 2), 0, 1),
                offset_ref[2 * at],
                offset_ref[2 * at + 1],
            )
            for k, value in enumerate(note):
                tail = jnp.where(lane == slot * fields + k, value, tail)
        tails[mask] = tail.astype(f32).astype(bf16)


def plan_slots(cap, owner_rows, offsets, extent):
    nbatch = lax.axis_size("batch")
    smem = pl.BlockSpec(memory_space=pltpu.SMEM)

    def kernel(*refs):
        plan_kernel(cap, nbatch, *refs)

    return pl.pallas_call(
        kernel,
        in_specs=[smem, smem],
        out_specs=(smem, pl.BlockSpec(memory_space=pltpu.VMEM)),
        out_shape=(
            jax.ShapeDtypeStruct((nbatch * cap,), jnp.int32),
            jax.ShapeDtypeStruct((nbatch, tail_rows, extent), bf16),
        ),
        scratch_shapes=[pltpu.SMEM((nbatch,), jnp.int32)],
    )(owner_rows.reshape(-1), offsets.reshape(-1))


def sender(send_sem, recv_sem):
    def send(source, target, device, *index):
        copy = pltpu.make_async_remote_copy(
            src_ref=source, dst_ref=target,
            send_sem=send_sem.at[index] if index else send_sem,
            recv_sem=recv_sem.at[index] if index else recv_sem,
            device_id=device, device_id_type=pl.DeviceIdType.MESH,
        )
        copy.start()
        return copy

    return send


def places():
    nbatch, ntile = lax.axis_size("batch"), lax.axis_size("tile")
    at, col = lax.axis_index("batch"), lax.axis_index("tile")

    def along_batch(r):
        return (lax.rem(at + r, nbatch), col)

    def along_tile(r):
        return (at, lax.rem(col + r, ntile))

    return nbatch, ntile, at, col, along_batch, along_tile


def greet():
    nbatch, ntile, _, _, along_batch, along_tile = places()
    barrier = pltpu.get_barrier_semaphore()
    mesh_id = pl.DeviceIdType.MESH
    for r in range(1, nbatch):
        pl.semaphore_signal(barrier, inc=1, device_id=along_batch(r), device_id_type=mesh_id)
    for r in range(1, ntile):
        pl.semaphore_signal(barrier, inc=1, device_id=along_tile(r), device_id_type=mesh_id)
    return lambda: pl.semaphore_wait(barrier, nbatch - 1 + ntile - 1)


def open_kernel(cap, index_ref, tails_ref, measured_ref, field_ref, sort_ref, *refs):
    nbatch, ntile, at, col, along_batch, along_tile = places()
    pays = refs[:nbatch]
    (
        got_ref, own_ref, other_ref, beside_ref, row_ref,
        pad, held, ready, edge, beside, row_out, row_in, other, got,
        load_sem, pay_sem, tile_sem, edge_sem, row_sem,
    ) = refs[nbatch:]
    slices, _, height, width = field_ref.shape
    planes = 2 * slices
    positions, extent = held.shape[0], held.shape[-1]
    loads = [
        pltpu.make_async_copy(
            field_ref.at[q // 2, q % 2], pad.at[q, pl.ds(8, height), :], load_sem.at[q]
        )
        for q in range(planes)
    ] + [
        pltpu.make_async_copy(measured_ref.at[p], held.at[p], load_sem.at[planes + p])
        for p in range(positions)
    ]
    for load in loads:
        load.start()
    everyone_in = greet()
    for load in loads[:planes]:
        load.wait()
    lane = lax.broadcasted_iota(jnp.int32, (height, lanes), 1)
    edges = jnp.zeros((height, lanes), f32)
    for q in range(planes):
        edges = jnp.where(lane == q, pad[q, 8 : 8 + height, width - 1 : width], edges)
        edges = jnp.where(lane == planes + q, pad[q, 8 : 8 + height, 0:1], edges)
    edge[...] = edges
    for q in range(planes):
        for j in range(width // lanes):
            cols = slice(j * lanes, (j + 1) * lanes)
            own_ref[q // 2, q % 2, j] = pad[q, 8 : 8 + height, cols].astype(bf16)
    everyone_in()
    send = sender(edge_sem.at[0], edge_sem.at[1])
    sides = [
        send(edge, beside.at[0], along_tile(1), 0),
        send(edge, beside.at[1], along_tile(ntile - 1), 1),
    ]
    sibling = (at + 1 - 2 * lax.rem(at, 2), col)
    tile_sent = sender(tile_sem.at[0], tile_sem.at[1])(own_ref, other, sibling)
    for load in loads[planes:]:
        load.wait()
    for p in range(positions):
        ready[p] = dot(held[p].astype(bf16), sort_ref[...]).astype(bf16)

    def fill(mask):
        for slot in range(cap):
            rows = slice(slot * extent, (slot + 1) * extent)
            pays[mask][rows] = ready[index_ref[mask * cap + slot]]
        pays[mask][cap * extent :] = tails_ref[mask]

    fill(1)
    pay_sent = sender(pay_sem.at[0], pay_sem.at[1])(pays[1], got, sibling)
    for copy in sides:
        copy.wait()
    for q in range(planes):
        first = beside[0, 0:1, q : q + 1]
        last = beside[1, height - 1 : height, planes + q : planes + q + 1]
        row_out[0, q : q + 1, :width] = pad[q, 8:9, :]
        row_out[0, q : q + 1, width:] = jnp.broadcast_to(first, (1, lanes))
        row_out[1, q : q + 1, :width] = pad[q, 7 + height : 8 + height, :]
        row_out[1, q : q + 1, width:] = jnp.broadcast_to(last, (1, lanes))
    send = sender(row_sem.at[0], row_sem.at[1])
    ends = [
        send(row_out.at[0], row_in.at[0], along_batch(nbatch - 1), 0),
        send(row_out.at[1], row_in.at[1], along_batch(1), 1),
    ]
    for mask in (0, *range(2, nbatch)):
        fill(mask)
    for copy in ends:
        copy.wait()
    beside_ref[...] = beside[...]
    row_ref[...] = row_in[...]
    tile_sent.wait()
    other_ref[...] = other[...]
    pay_sent.wait()
    got_ref[...] = got[...]


def open_up(cap, index, tails, intensities, field, sort):
    nbatch = lax.axis_size("batch")
    slices, _, height, width = field.shape
    planes = 2 * slices
    positions, extent = intensities.shape[0], intensities.shape[-1]
    vmem = pl.BlockSpec(memory_space=pltpu.VMEM)
    anywhere = pl.BlockSpec(memory_space=pl.ANY)
    dma = pltpu.SemaphoreType.DMA
    tile = (slices, 2, width // lanes, height, lanes)
    pay = (cap * extent + tail_rows, extent)

    def kernel(*refs):
        open_kernel(cap, *refs)

    return pl.pallas_call(
        kernel,
        in_specs=[pl.BlockSpec(memory_space=pltpu.SMEM), vmem, anywhere, anywhere, vmem],
        out_specs=[vmem] * (nbatch + 5),
        out_shape=[jax.ShapeDtypeStruct(pay, bf16)] * (nbatch + 1)
        + [jax.ShapeDtypeStruct(tile, bf16)] * 2
        + [
            jax.ShapeDtypeStruct((2, height, lanes), f32),
            jax.ShapeDtypeStruct((2, 8, width + lanes), f32),
        ],
        scratch_shapes=[
            pltpu.VMEM((planes, height + 16, width), f32),
            pltpu.VMEM((positions, extent, extent), f32),
            pltpu.VMEM((positions, extent, extent), bf16),
            pltpu.VMEM((height, lanes), f32),
            pltpu.VMEM((2, height, lanes), f32),
            pltpu.VMEM((2, 8, width + lanes), f32),
            pltpu.VMEM((2, 8, width + lanes), f32),
            pltpu.VMEM(tile, bf16),
            pltpu.VMEM(pay, bf16),
            dma((planes + positions,)),
            dma((2,)),
            dma((2,)),
            dma((2, 2)),
            dma((2, 2)),
        ],
        compiler_params=pltpu.CompilerParams(
            vmem_limit_bytes=40 * 1024 * 1024, collective_id=1, has_side_effects=True
        ),
    )(index, tails, intensities, field, sort)


def smooth_kernel(field_ref, beside, row_in, base_ref, pad, falls, rest):
    slices, _, height, width = field_ref.shape
    planes = 2 * slices
    for q in range(planes):
        pad[q, 8 : 8 + height, :] = field_ref[q // 2, q % 2]
    for q in range(planes):
        pad[q, 7:8, :] = row_in[1, q : q + 1, :width]
        pad[q, 8 + height : 9 + height, :] = row_in[0, q : q + 1, :width]

    def weighed(downs, rights):
        squares = sum(d * d for d in downs) + sum(d * d for d in rights)
        return lax.rsqrt(squares + tv_smooth)

    def flows(block):
        place = lax.broadcasted_iota(jnp.int32, (block, width), 1)
        for slab in range(slices):
            pair = (2 * slab, 2 * slab + 1)
            above = [pad[q, 7:8, :] for q in pair]
            corner = [row_in[1, q : q + 1, width : width + 1] for q in pair]
            downs = [pad[q, 8:9, :] - x for q, x in zip(pair, above)]
            rights = [
                jnp.where(place[:1] == width - 1, c, pltpu.roll(x, width - 1, 1)) - x
                for c, x in zip(corner, above)
            ]
            weight = weighed(downs, rights)
            for q, d in zip(pair, downs):
                falls[q, 7:8, :] = weight * d
            for start in range(0, height, block):
                here = [pad[q, 8 + start : 8 + start + block, :] for q in pair]
                below = [pad[q, 9 + start : 9 + start + block, :] for q in pair]
                edge_right = [
                    beside[1, start : start + block, planes + q : planes + q + 1] for q in pair
                ]
                downs = [b - x for b, x in zip(below, here)]
                rights = [
                    jnp.where(place == width - 1, e, pltpu.roll(x, width - 1, 1)) - x
                    for e, x in zip(edge_right, here)
                ]
                weight = weighed(downs, rights)
                left = [beside[0, start : start + block, q : q + 1] for q in pair]
                if start + block < height:
                    left_down = [beside[0, start + 1 : start + block + 1, q : q + 1] for q in pair]
                else:
                    left_down = [
                        jnp.concatenate(
                            [
                                beside[0, start + 1 : height, q : q + 1],
                                row_in[0, q : q + 1, width : width + 1],
                            ],
                            0,
                        )
                        for q in pair
                    ]
                left_rights = [x[:, :1] - l for x, l in zip(here, left)]
                left_weight = weighed([b - l for b, l in zip(left_down, left)], left_rights)
                for q, d, e, g in zip(pair, downs, rights, left_rights):
                    fall, run = weight * d, weight * e
                    before = jnp.where(place == 0, left_weight * g, pltpu.roll(run, 1, 1))
                    falls[q, 8 + start : 8 + start + block, :] = fall
                    rest[q, start : start + block, :] = before - run - fall

    flows(32)
    for q in range(planes):
        for j in range(width // lanes):
            cols = slice(j * lanes, (j + 1) * lanes)
            tv = falls[q, 7 : 7 + height, cols] + rest[q, :, cols]
            here = pad[q, 8 : 8 + height, cols]
            base_ref[q // 2, q % 2, :, cols] = here - update_rate * tv_weight * tv


def smooth(field, beside, row_in):
    slices, _, height, width = field.shape
    planes = 2 * slices
    vmem = pl.BlockSpec(memory_space=pltpu.VMEM)
    return pl.pallas_call(
        smooth_kernel,
        in_specs=[vmem] * 3,
        out_specs=vmem,
        out_shape=jax.ShapeDtypeStruct(field.shape, f32),
        scratch_shapes=[
            pltpu.VMEM((planes, height + 16, width), f32),
            pltpu.VMEM((planes, height + 8, width), f32),
            pltpu.VMEM((planes, height, width), f32),
        ],
        compiler_params=pltpu.CompilerParams(vmem_limit_bytes=24 * 1024 * 1024),
        cost_estimate=pl.CostEstimate(
            flops=60 * field.size, bytes_accessed=8 * field.size, transcendentals=field.size
        ),
    )(field, beside, row_in)


def finish_kernel(
    sums_ref, other_ref, total_ref, probe_ref, grad_ref, new_probe_ref,
    taken, mine, gathered, share, whole, sum_sem, gather_sem, share_sem, spread_sem,
):
    nbatch, ntile, at, col, along_batch, along_tile = places()
    extent = probe_ref.shape[-1]
    chunk = 2 * extent // nbatch
    everyone_in = greet()
    for part in range(2):
        mine[part * extent : (part + 1) * extent] = total_ref[part].astype(bf16)
    everyone_in()
    send = sender(gather_sem.at[0], gather_sem.at[1])
    gathers = []
    for r in range(1, nbatch):
        rows = pl.ds(lax.rem(at + r, nbatch) * chunk, chunk)
        gathers.append(send(mine.at[rows], gathered.at[r - 1], along_batch(r), r - 1))
    sibling = (at + 1 - 2 * lax.rem(at, 2), col)
    summed = sender(sum_sem.at[0], sum_sem.at[1])(other_ref, taken, sibling)
    for copy in gathers:
        copy.wait()
    part = mine[pl.ds(at * chunk, chunk)].astype(f32)
    for r in range(1, nbatch):
        part = part + gathered[r - 1].astype(f32)
    share[pl.ds(col, 1)] = part.astype(bf16)[None]
    send = sender(share_sem.at[0], share_sem.at[1])
    shares = [
        send(share.at[col], share.at[col], along_tile(r), r - 1) for r in range(1, ntile)
    ]
    summed.wait()
    slices, _, cols, _, _ = sums_ref.shape
    for slab in range(slices):
        for p in range(2):
            for j in range(cols):
                total = sums_ref[slab, p, j] + taken[slab, p, j].astype(f32)
                grad_ref[slab, p, :, j * lanes : (j + 1) * lanes] = total
    for copy in shares:
        copy.wait()
    final = share[0].astype(f32)
    for i in range(1, ntile):
        final = final + share[i].astype(f32)
    own_rows = pl.ds(at * chunk, chunk)
    whole[own_rows] = final.astype(bf16)
    send = sender(spread_sem.at[0], spread_sem.at[1])
    spreads = [
        send(whole.at[own_rows], whole.at[own_rows], along_batch(r), r - 1)
        for r in range(1, nbatch)
    ]
    for copy in spreads:
        copy.wait()
    for part in range(2):
        rows = slice(part * extent, (part + 1) * extent)
        new_probe_ref[part] = probe_ref[part].astype(f32) - probe_rate * whole[rows].astype(f32)


def finish(sums, other, total, probe, shape):
    nbatch, ntile = lax.axis_size("batch"), lax.axis_size("tile")
    extent = probe.shape[-1]
    chunk = 2 * extent // nbatch
    vmem = pl.BlockSpec(memory_space=pltpu.VMEM)
    dma = pltpu.SemaphoreType.DMA
    return pl.pallas_call(
        finish_kernel,
        in_specs=[vmem] * 4,
        out_specs=(vmem, vmem),
        out_shape=(
            jax.ShapeDtypeStruct(shape, f32),
            jax.ShapeDtypeStruct(probe.shape, f32),
        ),
        scratch_shapes=[
            pltpu.VMEM(other.shape, bf16),
            pltpu.VMEM((2 * extent, extent), bf16),
            pltpu.VMEM((nbatch - 1, chunk, extent), bf16),
            pltpu.VMEM((ntile, chunk, extent), bf16),
            pltpu.VMEM((2 * extent, extent), bf16),
            dma((2,)),
            dma((2, nbatch - 1)),
            dma((2, ntile - 1)),
            dma((2, nbatch - 1)),
        ],
        compiler_params=pltpu.CompilerParams(
            vmem_limit_bytes=20 * 1024 * 1024, collective_id=0, has_side_effects=True
        ),
        cost_estimate=pl.CostEstimate(
            flops=4 * sums.size, bytes_accessed=16 * sums.size, transcendentals=0
        ),
    )(sums, other, total, probe)


def on_device(object_field, probe_wave, intensities, owner_rows, offsets):
    extent = probe_wave.shape[-1]
    nbatch = lax.axis_size("batch")
    cap = max(2, 2 * intensities.shape[0] // nbatch)
    fixed = tables(extent)

    def swap(x, mask):
        return lax.ppermute(x, "batch", [(i, i ^ mask) for i in range(nbatch)])

    tabs, prop, sort = fixed
    index, tails = plan_slots(cap, owner_rows, offsets, extent)
    *pays, got, own, other, beside, row_in = open_up(
        cap, index, tails, intensities, object_field, sort
    )
    near = [swap(pays[m], m) for m in range(2, nbatch - 2)]

    def phase(group, carried, last=False):
        return visits(cap, group, own, other, probe_wave, (tabs, prop), carried, last)

    carried = phase((pays[0], got), ())
    base = smooth(object_field, beside, row_in)
    *carried, base, far_six, far_seven = lax.optimization_barrier(
        (*carried, base, pays[-2], pays[-1])
    )
    *near, far_six, far_seven = lax.optimization_barrier((*near, far_six, far_seven))
    far = [swap(far_six, nbatch - 2), swap(far_seven, nbatch - 1)]
    carried = phase(near, carried)
    carried = phase(far, carried, True)
    sums, returned, total = carried
    grad, new_probe = finish(sums, returned, total, probe_wave, object_field.shape)
    return (base - update_rate * grad, new_probe)


def solution(mesh):
    return jax.shard_map(
        on_device,
        mesh=mesh,
        in_specs=(
            P(None, None, "batch", "tile"),
            P(),
            P(("batch", "tile"), None, None),
            P(("batch", "tile"), None),
            P(("batch", "tile"), None),
        ),
        out_specs=(P(None, None, "batch", "tile"), P()),
        check_vma=False,
    )
```

```python
import math

import jax
import jax.numpy as jnp
import ml_dtypes
import numpy as np
from jax import lax
from jax.experimental import pallas as pl
from jax.experimental.pallas import tpu as pltpu
from jax.sharding import PartitionSpec as P

update_rate = 0.1
tv_weight = 12.0
tv_smooth = 1.0
probe_rate = 0.04
lanes = 128
block = 32
together_at_once = 3
fields = 4
tail_rows = 16
f32, bf16 = jnp.float32, jnp.bfloat16


def tables(extent):
    half = extent // 2
    counter = np.arange(extent)
    angles = (counter[:, None] * counter[None, :] % extent) * (2.0 * math.pi / extent)
    scaling = 1.0 / math.sqrt(extent)
    cos_table, sin_table = np.cos(angles) * scaling, -np.sin(angles) * scaling

    def packed(first):
        real, imag = cos_table[first::2, :half], sin_table[first::2, :half]
        return np.block([[real, -imag], [imag, real]])

    even, odd = packed(0), packed(1)
    order = np.concatenate([counter[0::2], counter[1::2]])
    squared = ((counter + half) % extent - half).astype(np.float64) ** 2
    phases = -(0.5 / extent) * (squared[:, None] + squared[order][None, :])
    sort = counter[:, None] == order[None, :]

    def whole(sine):
        return np.block([[cos_table, -sine], [sine, cos_table]])

    def as_bf16(x):
        return jnp.asarray(np.asarray(x).astype(np.float32).astype(ml_dtypes.bfloat16))

    return (
        (
            as_bf16(np.stack([whole(sin_table), whole(-sin_table)])),
            as_bf16(np.stack([even, odd, even.T, odd.T])),
        ),
        jnp.asarray(np.stack([np.cos(phases), np.sin(phases)]).astype(np.float32)),
        as_bf16(sort),
    )


def dot(a, b):
    return jnp.dot(a, b, preferred_element_type=f32)


def visit_stages(tile, row_at, col_at, measured, probe, tabs, prop, wide, summed, total, work):
    field, mid_near, mid_far, psi, trans = work
    left, tabs = tabs
    extent = field.shape[-1]
    half = extent // 2
    slices = trans.shape[0]
    even, odd, even_t, odd_t = (tabs.at[i] for i in range(4))
    rest = lax.rem(col_at, lanes)
    base = lax.div(col_at, lanes)
    back = lax.rem(lanes - rest, lanes)
    lane = lax.broadcasted_iota(jnp.int32, (block, lanes), 1)
    keep = lane < lanes - rest
    ahead = lane >= rest
    last = wide.shape[3] - 1
    spots = [jnp.minimum(base + j, last) for j in range(3)]
    halves = (slice(0, half), slice(half, extent))

    def cut(slab, part, r):
        rows = pl.ds(row_at + r, block)
        cols = [pltpu.roll(wide[tile, slab, part, spots[j], rows, :], back, 1) for j in range(3)]
        pair = [jnp.where(keep, cols[j], cols[j + 1]) for j in range(2)]
        for h in range(2):
            trans[slab, part, r:r + block, halves[h]] = pair[h]
        return pair

    def add(slab, part, r, pair):
        left, right = [pltpu.roll(x.astype(bf16).astype(f32), rest, 1) for x in pair]
        rows = pl.ds(row_at + r, block)
        summed[tile, slab, part, spots[0], rows, :] += jnp.where(ahead, left, 0.0)
        summed[tile, slab, part, spots[1], rows, :] += jnp.where(ahead, right, left)
        summed[tile, slab, part, spots[2], rows, :] += jnp.where(ahead, 0.0, right)

    def enter(r, real, imag):
        for k, x in enumerate((real, imag)):
            for g, at in enumerate((r, half + r)):
                rows = slice(k * extent + at, k * extent + at + block)
                for h in range(2):
                    field[rows, halves[h]] = x[g][h].astype(bf16)

    def place(r, h, real, imag):
        field[r : r + block, halves[h]] = real.astype(bf16)
        field[extent + r : extent + r + block, halves[h]] = imag.astype(bf16)

    def outward_left():
        for k in range(2):
            y = dot(left[0, k * extent : (k + 1) * extent], field[...])
            for r in range(0, extent, block):
                a, b = y[r : r + block, :half], y[r : r + block, half:]
                mid_near[r : r + block, halves[k]] = (a + b).astype(bf16)
                mid_far[r : r + block, halves[k]] = (a - b).astype(bf16)

    def outward_right(use):
        for h, (x, table) in enumerate(((mid_near, even_t), (mid_far, odd_t))):
            y = dot(x[...], table[...])
            for r in range(0, extent, block):
                use(r, h, y[r:r + block, :half], y[r:r + block, half:])

    def inward_left():
        for k in range(2):
            y = dot(left[1, k * extent : (k + 1) * extent], field[...])
            for r in range(0, extent, block):
                for h, to in enumerate((mid_near, mid_far)):
                    to[r : r + block, halves[k]] = y[r : r + block, halves[h]].astype(bf16)

    def inward_right(use):
        e = dot(mid_near[...], even[...])
        o = dot(mid_far[...], odd[...])
        for r in range(0, half, block):
            real, imag = [], []
            for at in (r, half + r):
                for into, c in ((real, halves[0]), (imag, halves[1])):
                    a, b = e[at:at + block, c], o[at:at + block, c]
                    into.append([a + b, a - b])
            use(r, real, imag)

    groups = lambda r: (r, half + r)

    def times(w, t):
        wr, wi = w
        tr, ti = t
        return wr * tr - wi * ti, wr * ti + wi * tr

    def first(r):
        out = [], []
        for at in groups(r):
            t = [cut(0, part, at) for part in range(2)]
            rows = slice(at, at + block)
            pair = [times([probe[part, rows, halves[h]] for part in range(2)], [t[part][h] for part in range(2)]) for h in range(2)]
            for part in range(2):
                out[part].append([p[part] for p in pair])
        enter(r, *out)

    for r in range(0, half, block):
        first(r)
    yield

    def kick(r, h, fr, fi):
        pr, pi = (prop[part, r:r + block, halves[h]] for part in range(2))
        place(r, h, pr * fr - pi * fi, pr * fi + pi * fr)

    def kick_back(r, h, bi, br):
        pr, pi = (prop[part, r:r + block, halves[h]] for part in range(2))
        place(r, h, pr * bi - pi * br, pr * br + pi * bi)

    def entering(slab):
        def use(r, real, imag):
            out = [], []
            for g, at in enumerate(groups(r)):
                rows = slice(at, at + block)
                t = [cut(slab, part, at) for part in range(2)]
                pair = []
                for h in range(2):
                    w = [x[g][h].astype(bf16).astype(f32) for x in (real, imag)]
                    for part in range(2):
                        psi[slab - 1, part, rows, halves[h]] = w[part]
                    pair.append(times(w, [t[part][h] for part in range(2)]))
                for part in range(2):
                    out[part].append([p[part] for p in pair])
            enter(r, *out)
        return use

    for slab in range(1, slices):
        outward_left()
        yield
        outward_right(kick)
        yield
        inward_left()
        yield
        inward_right(entering(slab))
        yield
    outward_left()
    yield

    def residual(r, h, fr, fi):
        misfit = 0.5 * (fr * fr + fi * fi - measured(r, h))
        place(r, h, misfit * fr, misfit * fi)

    outward_right(residual)
    yield
    inward_left()
    yield

    def leaving(slab, swapped):
        def use(r, real, imag):
            if swapped:
                real, imag = imag, real
            out = [], []
            for g, at in enumerate(groups(r)):
                rows = slice(at, at + block)
                grads, back_ = [], []
                for h in range(2):
                    gr, gi = real[g][h], imag[g][h]
                    if slab == 0:
                        wr, wi = (probe[part, rows, halves[h]] for part in range(2))
                    else:
                        wr, wi = (psi[slab - 1, part, rows, halves[h]] for part in range(2))
                    tr, ti = (trans[slab, part, rows, halves[h]] for part in range(2))
                    grads.append((gr * wr + gi * wi, gi * wr - gr * wi))
                    back_.append((gr * tr + gi * ti, gi * tr - gr * ti))
                for part in range(2):
                    add(slab, part, at, [x[part] for x in grads])
                    if slab == 0:
                        for h in range(2):
                            total[part, rows, halves[h]] += back_[h][part]
                    out[part].append([x[part] for x in back_])
            if slab > 0:
                enter(r, out[1], out[0])
        return use

    inward_right(leaving(slices - 1, False))
    yield
    for slab in range(slices - 1, 0, -1):
        outward_left()
        yield
        outward_right(kick_back)
        yield
        inward_left()
        yield
        inward_right(leaving(slab - 1, True))
        yield

def run_together(stages):
    stages = list(stages)
    live = [True] * len(stages)
    tick = 0
    while any(live):
        for i, s in enumerate(stages):
            if live[i] and tick >= i:
                try:
                    next(s)
                except StopIteration:
                    live[i] = False
        tick += 1


def visits_kernel(cap, first, last, sources, *refs):
    pays = refs[:sources]
    own_ref, other_ref, probe_ref, left_ref, tables_ref, prop_ref = refs[sources : sources + 6]
    carried = refs[sources + 6 : sources + 6 + (0 if first else 2)]
    rest = refs[sources + 6 + len(carried) :]
    if last:
        sums_out, other_out, total_ref, *rest, sums_ref = rest
    else:
        sums_ref, total_ref, *rest = rest
    wide, held, probe, notes, plan, listed, pay_sem, sem, *work = rest
    extent = probe_ref.shape[-1]
    copies = [
        pltpu.make_async_copy(pay, held.at[s], pay_sem.at[s]) for s, pay in enumerate(pays)
    ]
    for copy in copies:
        copy.start()
    for t, tile_ref in enumerate((own_ref, other_ref)):
        wide[t] = tile_ref[...].astype(f32)
    probe[...] = probe_ref[...].astype(f32)
    if first:
        sums_ref[...] = jnp.zeros_like(sums_ref)
        total_ref[...] = jnp.zeros_like(total_ref)
    else:
        sums_ref[...] = carried[0][...]
        total_ref[...] = carried[1][...]
    for copy in copies:
        copy.wait()
    for s in range(sources):
        tail = held[s, cap * extent : cap * extent + tail_rows, :lanes]
        notes[s * 8 : s * 8 + 8] = tail.astype(f32)[:8].astype(jnp.int32)
    copy = pltpu.make_async_copy(notes, plan, sem)
    copy.start()
    copy.wait()
    count = jnp.int32(0)
    for s in range(sources):
        for i in range(cap):
            listed[count] = s * cap + i
            count = count + plan[s * 8, i * fields]

    def one(k, lane):
        at = listed[k]
        source, slot = lax.div(at, cap), lax.rem(at, cap)
        tile, row_at, col_at = (plan[source * 8, slot * fields + j] for j in (1, 2, 3))

        def measured(r, h):
            rows = pl.ds(pl.multiple_of(slot * extent + r, block), block)
            return held[source, rows, h * lanes : (h + 1) * lanes].astype(f32)

        return visit_stages(
            tile, row_at, col_at, measured, probe, (left_ref, tables_ref), prop_ref,
            wide, sums_ref, total_ref, [w.at[lane] for w in work],
        )

    def together(i, carry):
        run_together([one(together_at_once * i + k, k) for k in range(together_at_once)])
        return carry

    def alone(k, carry):
        run_together([one(k, 0)])
        return carry

    groups = lax.div(count, together_at_once)
    lax.fori_loop(0, groups, together, 0)
    done = groups * together_at_once
    if last:
        left_over = lax.rem(count, together_at_once)

        @pl.when(left_over == 2)
        def _():
            run_together([one(done, 0), one(done + 1, 1)])

        done = done + jnp.where(left_over == 2, 2, 0)
    lax.fori_loop(done, count, alone, 0)
    if last:
        sums_out[...] = sums_ref[0]
        other_out[...] = sums_ref[1].astype(bf16)


def visits(cap, pays, own, other, probe, fixed, carried, last):
    (left, right), prop = fixed
    slices = own.shape[0]
    extent = probe.shape[-1]
    sources = len(pays)
    shape = (2, *own.shape)
    vmem = pl.BlockSpec(memory_space=pltpu.VMEM)

    def kernel(*refs):
        visits_kernel(cap, not carried, last, sources, *refs)

    operands = (*pays, own, other, probe, left, right, prop, *carried)
    return pl.pallas_call(
        kernel,
        in_specs=[pl.BlockSpec(memory_space=pl.ANY)] * sources
        + [vmem] * (len(operands) - sources),
        out_specs=[vmem] * (3 if last else 2),
        out_shape=(
            [jax.ShapeDtypeStruct(shape[1:], f32), jax.ShapeDtypeStruct(shape[1:], bf16)]
            if last
            else [jax.ShapeDtypeStruct(shape, f32)]
        )
        + [jax.ShapeDtypeStruct((2, extent, extent), f32)],
        scratch_shapes=[
            pltpu.VMEM(shape, f32),
            pltpu.VMEM((sources, *pays[0].shape), bf16),
            pltpu.VMEM(probe.shape, f32),
            pltpu.VMEM((8 * sources, lanes), jnp.int32),
            pltpu.SMEM((8 * sources, lanes), jnp.int32),
            pltpu.SMEM((sources * cap + 1,), jnp.int32),
            pltpu.SemaphoreType.DMA((sources,)),
            pltpu.SemaphoreType.DMA,
        ]
        + [pltpu.VMEM((together_at_once, 2 * extent, extent), bf16)]
        + [pltpu.VMEM((together_at_once, extent, extent), bf16)] * 2
        + [
            pltpu.VMEM((together_at_once, slices - 1, 2, extent, extent), f32),
            pltpu.VMEM((together_at_once, slices, 2, extent, extent), f32),
        ]
        + [pltpu.VMEM(shape, f32)] * last,
        compiler_params=pltpu.CompilerParams(vmem_limit_bytes=26 * 1024 * 1024),
        cost_estimate=pl.CostEstimate(
            flops=sources * cap * 3 * slices * 16 * extent**3,
            bytes_accessed=16 * 1024 * 1024,
            transcendentals=0,
        ),
    )(*operands)


def plan_kernel(cap, nbatch, owner_ref, offset_ref, index, tails, count):
    extent = tails.shape[-1]
    me = lax.axis_index("batch")

    def clear(i, carry):
        index[i] = -1
        return carry

    lax.fori_loop(0, nbatch * cap, clear, 0)

    def clear_count(i, carry):
        count[i] = 0
        return carry

    lax.fori_loop(0, nbatch, clear_count, 0)

    def place(p, carry):
        row = owner_ref[p]
        rank = count[row]
        count[row] = rank + 1
        bit = lax.rem(row, 2)
        dest = row - bit + lax.rem(rank + row + me, 2)
        slot = bit * (cap // 2) + lax.div(rank, 2)
        index[jnp.bitwise_xor(dest, me) * cap + slot] = p
        return carry

    lax.fori_loop(0, owner_ref.shape[0], place, 0)
    lane = lax.broadcasted_iota(jnp.int32, (tail_rows, extent), 1)
    for mask in range(nbatch):
        dest_bit = lax.rem(jnp.bitwise_xor(me, mask), 2)
        tail = jnp.zeros((tail_rows, extent), jnp.int32)
        for slot in range(cap):
            p = index[mask * cap + slot]
            at = jnp.maximum(p, 0)
            index[mask * cap + slot] = at
            note = (
                jnp.where(p >= 0, 1, 0),
                jnp.where(dest_bit == slot // (cap // 2), 0, 1),
                offset_ref[2 * at],
                offset_ref[2 * at + 1],
            )
            for k, value in enumerate(note):
                tail = jnp.where(lane == slot * fields + k, value, tail)
        tails[mask] = tail.astype(f32).astype(bf16)


def plan_slots(cap, owner_rows, offsets, extent):
    nbatch = lax.axis_size("batch")
    smem = pl.BlockSpec(memory_space=pltpu.SMEM)

    def kernel(*refs):
        plan_kernel(cap, nbatch, *refs)

    return pl.pallas_call(
        kernel,
        in_specs=[smem, smem],
        out_specs=(smem, pl.BlockSpec(memory_space=pltpu.VMEM)),
        out_shape=(
            jax.ShapeDtypeStruct((nbatch * cap,), jnp.int32),
            jax.ShapeDtypeStruct((nbatch, tail_rows, extent), bf16),
        ),
        scratch_shapes=[pltpu.SMEM((nbatch,), jnp.int32)],
        compiler_params=pltpu.CompilerParams(vmem_limit_bytes=4 * 1024 * 1024),
    )(owner_rows.reshape(-1), offsets.reshape(-1))


def sender(send_sem, recv_sem):
    def send(source, target, device, *index):
        copy = pltpu.make_async_remote_copy(
            src_ref=source, dst_ref=target,
            send_sem=send_sem.at[index] if index else send_sem,
            recv_sem=recv_sem.at[index] if index else recv_sem,
            device_id=device, device_id_type=pl.DeviceIdType.MESH,
        )
        copy.start()
        return copy

    return send


def places():
    nbatch, ntile = lax.axis_size("batch"), lax.axis_size("tile")
    at, col = lax.axis_index("batch"), lax.axis_index("tile")

    def along_batch(r):
        return (lax.rem(at + r, nbatch), col)

    def along_tile(r):
        return (at, lax.rem(col + r, ntile))

    return nbatch, ntile, at, col, along_batch, along_tile


def greet():
    nbatch, ntile, _, _, along_batch, along_tile = places()
    barrier = pltpu.get_barrier_semaphore()
    mesh_id = pl.DeviceIdType.MESH
    for r in range(1, nbatch):
        pl.semaphore_signal(barrier, inc=1, device_id=along_batch(r), device_id_type=mesh_id)
    for r in range(1, ntile):
        pl.semaphore_signal(barrier, inc=1, device_id=along_tile(r), device_id_type=mesh_id)
    return lambda: pl.semaphore_wait(barrier, nbatch - 1 + ntile - 1)


def greet_near():
    nbatch, ntile, _, _, along_batch, along_tile = places()
    barrier = pltpu.get_barrier_semaphore()
    mesh_id = pl.DeviceIdType.MESH
    near = (along_batch(1), along_batch(nbatch - 1), along_tile(1), along_tile(ntile - 1))
    for device in near:
        pl.semaphore_signal(barrier, inc=1, device_id=device, device_id_type=mesh_id)
    return lambda: pl.semaphore_wait(barrier, len(near))


def open_kernel(cap, index_ref, tails_ref, measured_ref, field_ref, sort_ref, *refs):
    nbatch, ntile, at, col, along_batch, along_tile = places()
    pays = refs[:nbatch]
    (
        got_ref, own_ref, other_ref, beside_ref, row_ref,
        pad, held, ready, edge, strip, beside, row_out, row_in, other, got,
        load_sem, pay_sem, tile_sem, edge_sem, row_sem,
    ) = refs[nbatch:]
    slices, _, height, width = field_ref.shape
    planes = 2 * slices
    positions, extent = held.shape[0], held.shape[-1]
    loads = [
        pltpu.make_async_copy(
            field_ref.at[q // 2, q % 2], pad.at[q, pl.ds(8, height), :], load_sem.at[q]
        )
        for q in range(planes)
    ] + [
        pltpu.make_async_copy(measured_ref.at[p], held.at[p], load_sem.at[planes + p])
        for p in range(positions)
    ]
    for load in loads:
        load.start()
    everyone_in = greet_near()
    for load in loads[:planes]:
        load.wait()
    lane = lax.broadcasted_iota(jnp.int32, (height, lanes), 1)
    edges = jnp.zeros((height, lanes), f32)
    for q in range(planes):
        edges = jnp.where(lane == q, pad[q, 8 : 8 + height, width - 1 : width], edges)
        edges = jnp.where(lane == planes + q, pad[q, 8 : 8 + height, 0:1], edges)
    edge[...] = edges.T[: edge.shape[0]]
    for q in range(planes):
        for j in range(width // lanes):
            cols = slice(j * lanes, (j + 1) * lanes)
            own_ref[q // 2, q % 2, j] = pad[q, 8 : 8 + height, cols].astype(bf16)
    everyone_in()
    send = sender(edge_sem.at[0], edge_sem.at[1])
    sides = [
        send(edge, strip.at[0], along_tile(1), 0),
        send(edge, strip.at[1], along_tile(ntile - 1), 1),
    ]
    sibling = (at + 1 - 2 * lax.rem(at, 2), col)
    tile_sent = sender(tile_sem.at[0], tile_sem.at[1])(own_ref, other, sibling)
    for load in loads[planes:]:
        load.wait()
    for p in range(positions):
        ready[p] = dot(held[p].astype(bf16), sort_ref[...]).astype(bf16)

    def fill(mask):
        for slot in range(cap):
            rows = slice(slot * extent, (slot + 1) * extent)
            pays[mask][rows] = ready[index_ref[mask * cap + slot]]
        pays[mask][cap * extent :] = tails_ref[mask]

    fill(1)
    pay_sent = sender(pay_sem.at[0], pay_sem.at[1])(pays[1], got, sibling)
    for copy in sides:
        copy.wait()
    blank = jnp.zeros((lanes - strip.shape[1], height), f32)
    for side in range(2):
        beside[side] = jnp.concatenate([strip[side], blank], 0).T
    for q in range(planes):
        first = beside[0, 0:1, q : q + 1]
        last = beside[1, height - 1 : height, planes + q : planes + q + 1]
        row_out[0, q : q + 1, :width] = pad[q, 8:9, :]
        row_out[0, q : q + 1, width:] = jnp.broadcast_to(first, (1, lanes))
        row_out[1, q : q + 1, :width] = pad[q, 7 + height : 8 + height, :]
        row_out[1, q : q + 1, width:] = jnp.broadcast_to(last, (1, lanes))
    send = sender(row_sem.at[0], row_sem.at[1])
    ends = [
        send(row_out.at[0], row_in.at[0], along_batch(nbatch - 1), 0),
        send(row_out.at[1], row_in.at[1], along_batch(1), 1),
    ]
    for mask in (0, *range(2, nbatch)):
        fill(mask)
    for copy in ends:
        copy.wait()
    beside_ref[...] = beside[...]
    row_ref[...] = row_in[...]
    tile_sent.wait()
    other_ref[...] = other[...]
    pay_sent.wait()
    got_ref[...] = got[...]


def open_up(cap, index, tails, intensities, field, sort):
    nbatch = lax.axis_size("batch")
    slices, _, height, width = field.shape
    planes = 2 * slices
    strip_rows = -(-2 * planes // 8) * 8
    positions, extent = intensities.shape[0], intensities.shape[-1]
    vmem = pl.BlockSpec(memory_space=pltpu.VMEM)
    hbm = pl.BlockSpec(memory_space=pltpu.HBM)
    dma = pltpu.SemaphoreType.DMA
    tile = (slices, 2, width // lanes, height, lanes)
    pay = (cap * extent + tail_rows, extent)

    def kernel(*refs):
        open_kernel(cap, *refs)

    return pl.pallas_call(
        kernel,
        in_specs=[pl.BlockSpec(memory_space=pltpu.SMEM), vmem, hbm, hbm, vmem],
        out_specs=[vmem] * (nbatch + 5),
        out_shape=[jax.ShapeDtypeStruct(pay, bf16)] * (nbatch + 1)
        + [jax.ShapeDtypeStruct(tile, bf16)] * 2
        + [
            jax.ShapeDtypeStruct((2, height, lanes), f32),
            jax.ShapeDtypeStruct((2, 8, width + lanes), f32),
        ],
        scratch_shapes=[
            pltpu.VMEM((planes, height + 16, width), f32),
            pltpu.VMEM((positions, extent, extent), f32),
            pltpu.VMEM((positions, extent, extent), bf16),
            pltpu.VMEM((strip_rows, height), f32),
            pltpu.VMEM((2, strip_rows, height), f32),
            pltpu.VMEM((2, height, lanes), f32),
            pltpu.VMEM((2, 8, width + lanes), f32),
            pltpu.VMEM((2, 8, width + lanes), f32),
            pltpu.VMEM(tile, bf16),
            pltpu.VMEM(pay, bf16),
            dma((planes + positions,)),
            dma((2,)),
            dma((2,)),
            dma((2, 2)),
            dma((2, 2)),
        ],
        compiler_params=pltpu.CompilerParams(
            vmem_limit_bytes=40 * 1024 * 1024, collective_id=1, has_side_effects=True
        ),
    )(index, tails, intensities, field, sort)


def smooth_kernel(field_ref, beside, row_in, base_ref, pad, falls, rest):
    slices, _, height, width = field_ref.shape
    planes = 2 * slices
    for q in range(planes):
        pad[q, 8 : 8 + height, :] = field_ref[q // 2, q % 2]
    for q in range(planes):
        pad[q, 7:8, :] = row_in[1, q : q + 1, :width]
        pad[q, 8 + height : 9 + height, :] = row_in[0, q : q + 1, :width]

    def weighed(downs, rights):
        squares = sum(d * d for d in downs) + sum(d * d for d in rights)
        return lax.rsqrt(squares + tv_smooth)

    def flows(block):
        place = lax.broadcasted_iota(jnp.int32, (block, width), 1)
        for slab in range(slices):
            pair = (2 * slab, 2 * slab + 1)
            above = [pad[q, 7:8, :] for q in pair]
            corner = [row_in[1, q : q + 1, width : width + 1] for q in pair]
            downs = [pad[q, 8:9, :] - x for q, x in zip(pair, above)]
            rights = [
                jnp.where(place[:1] == width - 1, c, pltpu.roll(x, width - 1, 1)) - x
                for c, x in zip(corner, above)
            ]
            weight = weighed(downs, rights)
            for q, d in zip(pair, downs):
                falls[q, 7:8, :] = weight * d
            for start in range(0, height, block):
                here = [pad[q, 8 + start : 8 + start + block, :] for q in pair]
                below = [pad[q, 9 + start : 9 + start + block, :] for q in pair]
                edge_right = [
                    beside[1, start : start + block, planes + q : planes + q + 1] for q in pair
                ]
                downs = [b - x for b, x in zip(below, here)]
                rights = [
                    jnp.where(place == width - 1, e, pltpu.roll(x, width - 1, 1)) - x
                    for e, x in zip(edge_right, here)
                ]
                weight = weighed(downs, rights)
                left = [beside[0, start : start + block, q : q + 1] for q in pair]
                if start + block < height:
                    left_down = [beside[0, start + 1 : start + block + 1, q : q + 1] for q in pair]
                else:
                    left_down = [
                        jnp.concatenate(
                            [
                                beside[0, start + 1 : height, q : q + 1],
                                row_in[0, q : q + 1, width : width + 1],
                            ],
                            0,
                        )
                        for q in pair
                    ]
                left_rights = [x[:, :1] - l for x, l in zip(here, left)]
                left_weight = weighed([b - l for b, l in zip(left_down, left)], left_rights)
                for q, d, e, g in zip(pair, downs, rights, left_rights):
                    fall, run = weight * d, weight * e
                    before = jnp.where(place == 0, left_weight * g, pltpu.roll(run, 1, 1))
                    falls[q, 8 + start : 8 + start + block, :] = fall
                    rest[q, start : start + block, :] = before - run - fall

    flows(32)
    for q in range(planes):
        for j in range(width // lanes):
            cols = slice(j * lanes, (j + 1) * lanes)
            tv = falls[q, 7 : 7 + height, cols] + rest[q, :, cols]
            here = pad[q, 8 : 8 + height, cols]
            base_ref[q // 2, q % 2, :, cols] = here - update_rate * tv_weight * tv


def smooth(field, beside, row_in):
    slices, _, height, width = field.shape
    planes = 2 * slices
    vmem = pl.BlockSpec(memory_space=pltpu.VMEM)
    return pl.pallas_call(
        smooth_kernel,
        in_specs=[vmem] * 3,
        out_specs=vmem,
        out_shape=jax.ShapeDtypeStruct(field.shape, f32),
        scratch_shapes=[
            pltpu.VMEM((planes, height + 16, width), f32),
            pltpu.VMEM((planes, height + 8, width), f32),
            pltpu.VMEM((planes, height, width), f32),
        ],
        compiler_params=pltpu.CompilerParams(vmem_limit_bytes=24 * 1024 * 1024),
        cost_estimate=pl.CostEstimate(
            flops=60 * field.size, bytes_accessed=8 * field.size, transcendentals=field.size
        ),
    )(field, beside, row_in)


def finish_kernel(
    sums_ref, other_ref, total_ref, probe_ref, grad_ref, new_probe_ref,
    taken, mine, gathered, share, whole, sum_sem, gather_sem, share_sem, spread_sem,
):
    nbatch, ntile, at, col, along_batch, along_tile = places()
    extent = probe_ref.shape[-1]
    chunk = 2 * extent // nbatch
    everyone_in = greet()
    for part in range(2):
        mine[part * extent : (part + 1) * extent] = total_ref[part].astype(bf16)
    everyone_in()
    send = sender(gather_sem.at[0], gather_sem.at[1])
    gathers = []
    for r in range(1, nbatch):
        rows = pl.ds(lax.rem(at + r, nbatch) * chunk, chunk)
        gathers.append(send(mine.at[rows], gathered.at[r - 1], along_batch(r), r - 1))
    sibling = (at + 1 - 2 * lax.rem(at, 2), col)
    summed = sender(sum_sem.at[0], sum_sem.at[1])(other_ref, taken, sibling)
    for copy in gathers:
        copy.wait()
    part = mine[pl.ds(at * chunk, chunk)].astype(f32)
    for r in range(1, nbatch):
        part = part + gathered[r - 1].astype(f32)
    share[pl.ds(col, 1)] = part.astype(bf16)[None]
    send = sender(share_sem.at[0], share_sem.at[1])
    shares = [
        send(share.at[col], share.at[col], along_tile(r), r - 1) for r in range(1, ntile)
    ]
    summed.wait()
    slices, _, cols, _, _ = sums_ref.shape
    for slab in range(slices):
        for p in range(2):
            for j in range(cols):
                total = sums_ref[slab, p, j] + taken[slab, p, j].astype(f32)
                grad_ref[slab, p, :, j * lanes : (j + 1) * lanes] = total
    for copy in shares:
        copy.wait()
    final = share[0].astype(f32)
    for i in range(1, ntile):
        final = final + share[i].astype(f32)
    own_rows = pl.ds(at * chunk, chunk)
    whole[own_rows] = final.astype(bf16)
    send = sender(spread_sem.at[0], spread_sem.at[1])
    spreads = [
        send(whole.at[own_rows], whole.at[own_rows], along_batch(r), r - 1)
        for r in range(1, nbatch)
    ]
    for copy in spreads:
        copy.wait()
    for part in range(2):
        rows = slice(part * extent, (part + 1) * extent)
        new_probe_ref[part] = probe_ref[part].astype(f32) - probe_rate * whole[rows].astype(f32)


def finish(sums, other, total, probe, shape):
    nbatch, ntile = lax.axis_size("batch"), lax.axis_size("tile")
    extent = probe.shape[-1]
    chunk = 2 * extent // nbatch
    vmem = pl.BlockSpec(memory_space=pltpu.VMEM)
    dma = pltpu.SemaphoreType.DMA
    return pl.pallas_call(
        finish_kernel,
        in_specs=[vmem] * 4,
        out_specs=(vmem, vmem),
        out_shape=(
            jax.ShapeDtypeStruct(shape, f32),
            jax.ShapeDtypeStruct(probe.shape, f32),
        ),
        scratch_shapes=[
            pltpu.VMEM(other.shape, bf16),
            pltpu.VMEM((2 * extent, extent), bf16),
            pltpu.VMEM((nbatch - 1, chunk, extent), bf16),
            pltpu.VMEM((ntile, chunk, extent), bf16),
            pltpu.VMEM((2 * extent, extent), bf16),
            dma((2,)),
            dma((2, nbatch - 1)),
            dma((2, ntile - 1)),
            dma((2, nbatch - 1)),
        ],
        compiler_params=pltpu.CompilerParams(
            vmem_limit_bytes=20 * 1024 * 1024, collective_id=0, has_side_effects=True
        ),
        cost_estimate=pl.CostEstimate(
            flops=4 * sums.size, bytes_accessed=16 * sums.size, transcendentals=0
        ),
    )(sums, other, total, probe)


def on_device(object_field, probe_wave, intensities, owner_rows, offsets):
    extent = probe_wave.shape[-1]
    nbatch = lax.axis_size("batch")
    cap = max(2, 2 * intensities.shape[0] // nbatch)
    fixed = tables(extent)

    def swap(x, mask):
        return lax.ppermute(x, "batch", [(i, i ^ mask) for i in range(nbatch)])

    tabs, prop, sort = fixed
    index, tails = plan_slots(cap, owner_rows, offsets, extent)
    *pays, got, own, other, beside, row_in = open_up(
        cap, index, tails, intensities, object_field, sort
    )
    near = [swap(pays[m], m) for m in range(2, nbatch - 2)]

    def phase(group, carried, last=False):
        return visits(cap, group, own, other, probe_wave, (tabs, prop), carried, last)

    carried = phase((pays[0], got), ())
    base = smooth(object_field, beside, row_in)
    *carried, base, far_six, far_seven = lax.optimization_barrier(
        (*carried, base, pays[-2], pays[-1])
    )
    *near, far_six, far_seven = lax.optimization_barrier((*near, far_six, far_seven))
    far = [swap(far_six, nbatch - 2), swap(far_seven, nbatch - 1)]
    carried = phase(near, carried)
    carried = phase(far, carried, True)
    sums, returned, total = carried
    grad, new_probe = finish(sums, returned, total, probe_wave, object_field.shape)
    return (base - update_rate * grad, new_probe)


def solution(mesh):
    return jax.shard_map(
        on_device,
        mesh=mesh,
        in_specs=(
            P(None, None, "batch", "tile"),
            P(),
            P(("batch", "tile"), None, None),
            P(("batch", "tile"), None),
            P(("batch", "tile"), None),
        ),
        out_specs=(P(None, None, "batch", "tile"), P()),
        check_vma=False,
    )
```

```python
import math

import jax
import jax.numpy as jnp
import ml_dtypes
import numpy as np
from jax import lax
from jax.experimental import pallas as pl
from jax.experimental.pallas import tpu as pltpu
from jax.sharding import PartitionSpec as P

update_rate = 0.1
tv_weight = 12.0
tv_smooth = 1.0
probe_rate = 0.04
lanes = 128
block = 32
together_at_once = 3
fields = 4
tail_rows = 16
f32, bf16 = jnp.float32, jnp.bfloat16


def tables(extent):
    half = extent // 2
    counter = np.arange(extent)
    angles = (counter[:, None] * counter[None, :] % extent) * (2.0 * math.pi / extent)
    scaling = 1.0 / math.sqrt(extent)
    cos_table, sin_table = np.cos(angles) * scaling, -np.sin(angles) * scaling

    def packed(first):
        real, imag = cos_table[first::2, :half], sin_table[first::2, :half]
        return np.block([[real, -imag], [imag, real]])

    even, odd = packed(0), packed(1)
    order = np.concatenate([counter[0::2], counter[1::2]])
    squared = ((counter + half) % extent - half).astype(np.float64) ** 2
    phases = -(0.5 / extent) * (squared[:, None] + squared[order][None, :])
    sort = counter[:, None] == order[None, :]

    def whole(sine):
        return np.block([[cos_table, -sine], [sine, cos_table]])

    def as_bf16(x):
        return jnp.asarray(np.asarray(x).astype(np.float32).astype(ml_dtypes.bfloat16))

    return (
        (
            as_bf16(np.stack([whole(sin_table), whole(-sin_table)])),
            as_bf16(np.stack([even, odd, even.T, odd.T])),
        ),
        jnp.asarray(np.stack([np.cos(phases), np.sin(phases)]).astype(np.float32)),
        as_bf16(sort),
    )


def dot(a, b):
    return jnp.dot(a, b, preferred_element_type=f32)


def visit_stages(tile, row_at, col_at, measured, probe, tabs, prop, wide, summed, total, work):
    field, mid_near, mid_far, psi, trans = work
    left, tabs = tabs
    extent = field.shape[-1]
    half = extent // 2
    slices = trans.shape[0]
    even, odd, even_t, odd_t = (tabs.at[i] for i in range(4))
    rest = lax.rem(col_at, lanes)
    base = lax.div(col_at, lanes)
    back = lax.rem(lanes - rest, lanes)
    lane = lax.broadcasted_iota(jnp.int32, (block, lanes), 1)
    keep = lane < lanes - rest
    ahead = lane >= rest
    last = wide.shape[3] - 1
    spots = [jnp.minimum(base + j, last) for j in range(3)]
    halves = (slice(0, half), slice(half, extent))

    def cut(slab, part, r):
        rows = pl.ds(row_at + r, block)
        cols = [pltpu.roll(wide[tile, slab, part, spots[j], rows, :], back, 1) for j in range(3)]
        pair = [jnp.where(keep, cols[j], cols[j + 1]) for j in range(2)]
        for h in range(2):
            trans[slab, part, r:r + block, halves[h]] = pair[h]
        return pair

    def add(slab, part, r, pair):
        left, right = [pltpu.roll(x.astype(bf16).astype(f32), rest, 1) for x in pair]
        rows = pl.ds(row_at + r, block)
        summed[tile, slab, part, spots[0], rows, :] += jnp.where(ahead, left, 0.0)
        summed[tile, slab, part, spots[1], rows, :] += jnp.where(ahead, right, left)
        summed[tile, slab, part, spots[2], rows, :] += jnp.where(ahead, 0.0, right)

    def enter(r, real, imag):
        for k, x in enumerate((real, imag)):
            for g, at in enumerate((r, half + r)):
                rows = slice(k * extent + at, k * extent + at + block)
                for h in range(2):
                    field[rows, halves[h]] = x[g][h].astype(bf16)

    def place(r, h, real, imag):
        field[r : r + block, halves[h]] = real.astype(bf16)
        field[extent + r : extent + r + block, halves[h]] = imag.astype(bf16)

    def outward_left():
        for k in range(2):
            y = dot(left[0, k * extent : (k + 1) * extent], field[...])
            for r in range(0, extent, block):
                a, b = y[r : r + block, :half], y[r : r + block, half:]
                mid_near[r : r + block, halves[k]] = (a + b).astype(bf16)
                mid_far[r : r + block, halves[k]] = (a - b).astype(bf16)

    def outward_right(use):
        for h, (x, table) in enumerate(((mid_near, even_t), (mid_far, odd_t))):
            y = dot(x[...], table[...])
            for r in range(0, extent, block):
                use(r, h, y[r:r + block, :half], y[r:r + block, half:])

    def inward_left():
        for k in range(2):
            y = dot(left[1, k * extent : (k + 1) * extent], field[...])
            for r in range(0, extent, block):
                for h, to in enumerate((mid_near, mid_far)):
                    to[r : r + block, halves[k]] = y[r : r + block, halves[h]].astype(bf16)

    def inward_right(use):
        e = dot(mid_near[...], even[...])
        o = dot(mid_far[...], odd[...])
        for r in range(0, half, block):
            real, imag = [], []
            for at in (r, half + r):
                for into, c in ((real, halves[0]), (imag, halves[1])):
                    a, b = e[at:at + block, c], o[at:at + block, c]
                    into.append([a + b, a - b])
            use(r, real, imag)

    groups = lambda r: (r, half + r)

    def times(w, t):
        wr, wi = w
        tr, ti = t
        return wr * tr - wi * ti, wr * ti + wi * tr

    def first(r):
        out = [], []
        for at in groups(r):
            t = [cut(0, part, at) for part in range(2)]
            rows = slice(at, at + block)
            pair = [times([probe[part, rows, halves[h]] for part in range(2)], [t[part][h] for part in range(2)]) for h in range(2)]
            for part in range(2):
                out[part].append([p[part] for p in pair])
        enter(r, *out)

    for r in range(0, half, block):
        first(r)
    yield

    def kick(r, h, fr, fi):
        pr, pi = (prop[part, r:r + block, halves[h]] for part in range(2))
        place(r, h, pr * fr - pi * fi, pr * fi + pi * fr)

    def kick_back(r, h, bi, br):
        pr, pi = (prop[part, r:r + block, halves[h]] for part in range(2))
        place(r, h, pr * bi - pi * br, pr * br + pi * bi)

    def entering(slab):
        def use(r, real, imag):
            out = [], []
            for g, at in enumerate(groups(r)):
                rows = slice(at, at + block)
                t = [cut(slab, part, at) for part in range(2)]
                pair = []
                for h in range(2):
                    w = [x[g][h].astype(bf16).astype(f32) for x in (real, imag)]
                    for part in range(2):
                        psi[slab - 1, part, rows, halves[h]] = w[part]
                    pair.append(times(w, [t[part][h] for part in range(2)]))
                for part in range(2):
                    out[part].append([p[part] for p in pair])
            enter(r, *out)
        return use

    for slab in range(1, slices):
        outward_left()
        yield
        outward_right(kick)
        yield
        inward_left()
        yield
        inward_right(entering(slab))
        yield
    outward_left()
    yield

    def residual(r, h, fr, fi):
        misfit = 0.5 * (fr * fr + fi * fi - measured(r, h))
        place(r, h, misfit * fr, misfit * fi)

    outward_right(residual)
    yield
    inward_left()
    yield

    def leaving(slab, swapped):
        def use(r, real, imag):
            if swapped:
                real, imag = imag, real
            out = [], []
            for g, at in enumerate(groups(r)):
                rows = slice(at, at + block)
                grads, back_ = [], []
                for h in range(2):
                    gr, gi = real[g][h], imag[g][h]
                    if slab == 0:
                        wr, wi = (probe[part, rows, halves[h]] for part in range(2))
                    else:
                        wr, wi = (psi[slab - 1, part, rows, halves[h]] for part in range(2))
                    tr, ti = (trans[slab, part, rows, halves[h]] for part in range(2))
                    grads.append((gr * wr + gi * wi, gi * wr - gr * wi))
                    back_.append((gr * tr + gi * ti, gi * tr - gr * ti))
                for part in range(2):
                    add(slab, part, at, [x[part] for x in grads])
                    if slab == 0:
                        for h in range(2):
                            total[part, rows, halves[h]] += back_[h][part]
                    out[part].append([x[part] for x in back_])
            if slab > 0:
                enter(r, out[1], out[0])
        return use

    inward_right(leaving(slices - 1, False))
    yield
    for slab in range(slices - 1, 0, -1):
        outward_left()
        yield
        outward_right(kick_back)
        yield
        inward_left()
        yield
        inward_right(leaving(slab - 1, True))
        yield

def run_together(stages):
    stages = list(stages)
    live = [True] * len(stages)
    tick = 0
    while any(live):
        for i, s in enumerate(stages):
            if live[i] and tick >= i:
                try:
                    next(s)
                except StopIteration:
                    live[i] = False
        tick += 1


def visits_kernel(cap, first, last, sources, *refs):
    pays = refs[:sources]
    own_ref, other_ref, probe_ref, left_ref, tables_ref, prop_ref = refs[sources : sources + 6]
    carried = refs[sources + 6 : sources + 6 + (0 if first else 2)]
    rest = refs[sources + 6 + len(carried) :]
    if last:
        sums_out, other_out, total_ref, *rest, sums_ref = rest
    else:
        sums_ref, total_ref, *rest = rest
    wide, held, probe, notes, plan, listed, pay_sem, sem, *work = rest
    extent = probe_ref.shape[-1]
    copies = [
        pltpu.make_async_copy(pay, held.at[s], pay_sem.at[s]) for s, pay in enumerate(pays)
    ]
    for copy in copies:
        copy.start()
    for t, tile_ref in enumerate((own_ref, other_ref)):
        wide[t] = tile_ref[...].astype(f32)
    probe[...] = probe_ref[...].astype(f32)
    if first:
        sums_ref[...] = jnp.zeros_like(sums_ref)
        total_ref[...] = jnp.zeros_like(total_ref)
    else:
        sums_ref[...] = carried[0][...]
        total_ref[...] = carried[1][...]
    for copy in copies:
        copy.wait()
    for s in range(sources):
        tail = held[s, cap * extent : cap * extent + tail_rows, :lanes]
        notes[s * 8 : s * 8 + 8] = tail.astype(f32)[:8].astype(jnp.int32)
    copy = pltpu.make_async_copy(notes, plan, sem)
    copy.start()
    copy.wait()
    count = jnp.int32(0)
    for s in range(sources):
        for i in range(cap):
            listed[count] = s * cap + i
            count = count + plan[s * 8, i * fields]

    def one(k, lane):
        at = listed[k]
        source, slot = lax.div(at, cap), lax.rem(at, cap)
        tile, row_at, col_at = (plan[source * 8, slot * fields + j] for j in (1, 2, 3))

        def measured(r, h):
            rows = pl.ds(pl.multiple_of(slot * extent + r, block), block)
            return held[source, rows, h * lanes : (h + 1) * lanes].astype(f32)

        return visit_stages(
            tile, row_at, col_at, measured, probe, (left_ref, tables_ref), prop_ref,
            wide, sums_ref, total_ref, [w.at[lane] for w in work],
        )

    def together(i, carry):
        run_together([one(together_at_once * i + k, k) for k in range(together_at_once)])
        return carry

    def alone(k, carry):
        run_together([one(k, 0)])
        return carry

    groups = lax.div(count, together_at_once)
    lax.fori_loop(0, groups, together, 0)
    lax.fori_loop(groups * together_at_once, count, alone, 0)
    if last:
        sums_out[...] = sums_ref[0]
        other_out[...] = sums_ref[1].astype(bf16)


def visits(cap, pays, own, other, probe, fixed, carried, last):
    (left, right), prop = fixed
    slices = own.shape[0]
    extent = probe.shape[-1]
    sources = len(pays)
    shape = (2, *own.shape)
    vmem = pl.BlockSpec(memory_space=pltpu.VMEM)

    def kernel(*refs):
        visits_kernel(cap, not carried, last, sources, *refs)

    operands = (*pays, own, other, probe, left, right, prop, *carried)
    return pl.pallas_call(
        kernel,
        in_specs=[pl.BlockSpec(memory_space=pl.ANY)] * sources
        + [vmem] * (len(operands) - sources),
        out_specs=[vmem] * (3 if last else 2),
        out_shape=(
            [jax.ShapeDtypeStruct(shape[1:], f32), jax.ShapeDtypeStruct(shape[1:], bf16)]
            if last
            else [jax.ShapeDtypeStruct(shape, f32)]
        )
        + [jax.ShapeDtypeStruct((2, extent, extent), f32)],
        scratch_shapes=[
            pltpu.VMEM(shape, f32),
            pltpu.VMEM((sources, *pays[0].shape), bf16),
            pltpu.VMEM(probe.shape, f32),
            pltpu.VMEM((8 * sources, lanes), jnp.int32),
            pltpu.SMEM((8 * sources, lanes), jnp.int32),
            pltpu.SMEM((sources * cap + 1,), jnp.int32),
            pltpu.SemaphoreType.DMA((sources,)),
            pltpu.SemaphoreType.DMA,
        ]
        + [pltpu.VMEM((together_at_once, 2 * extent, extent), bf16)]
        + [pltpu.VMEM((together_at_once, extent, extent), bf16)] * 2
        + [
            pltpu.VMEM((together_at_once, slices - 1, 2, extent, extent), f32),
            pltpu.VMEM((together_at_once, slices, 2, extent, extent), f32),
        ]
        + [pltpu.VMEM(shape, f32)] * last,
        compiler_params=pltpu.CompilerParams(vmem_limit_bytes=26 * 1024 * 1024),
        cost_estimate=pl.CostEstimate(
            flops=sources * cap * 3 * slices * 16 * extent**3,
            bytes_accessed=16 * 1024 * 1024,
            transcendentals=0,
        ),
    )(*operands)


def plan_kernel(cap, nbatch, owner_ref, offset_ref, index, tails, count):
    extent = tails.shape[-1]
    me = lax.axis_index("batch")

    def clear(i, carry):
        index[i] = -1
        return carry

    lax.fori_loop(0, nbatch * cap, clear, 0)

    def clear_count(i, carry):
        count[i] = 0
        return carry

    lax.fori_loop(0, nbatch, clear_count, 0)

    def place(p, carry):
        row = owner_ref[p]
        rank = count[row]
        count[row] = rank + 1
        bit = lax.rem(row, 2)
        dest = row - bit + lax.rem(rank + row + me, 2)
        slot = bit * (cap // 2) + lax.div(rank, 2)
        index[jnp.bitwise_xor(dest, me) * cap + slot] = p
        return carry

    lax.fori_loop(0, owner_ref.shape[0], place, 0)
    lane = lax.broadcasted_iota(jnp.int32, (tail_rows, extent), 1)
    for mask in range(nbatch):
        dest_bit = lax.rem(jnp.bitwise_xor(me, mask), 2)
        tail = jnp.zeros((tail_rows, extent), jnp.int32)
        for slot in range(cap):
            p = index[mask * cap + slot]
            at = jnp.maximum(p, 0)
            index[mask * cap + slot] = at
            note = (
                jnp.where(p >= 0, 1, 0),
                jnp.where(dest_bit == slot // (cap // 2), 0, 1),
                offset_ref[2 * at],
                offset_ref[2 * at + 1],
            )
            for k, value in enumerate(note):
                tail = jnp.where(lane == slot * fields + k, value, tail)
        tails[mask] = tail.astype(f32).astype(bf16)


def plan_slots(cap, owner_rows, offsets, extent):
    nbatch = lax.axis_size("batch")
    smem = pl.BlockSpec(memory_space=pltpu.SMEM)

    def kernel(*refs):
        plan_kernel(cap, nbatch, *refs)

    return pl.pallas_call(
        kernel,
        in_specs=[smem, smem],
        out_specs=(smem, pl.BlockSpec(memory_space=pltpu.VMEM)),
        out_shape=(
            jax.ShapeDtypeStruct((nbatch * cap,), jnp.int32),
            jax.ShapeDtypeStruct((nbatch, tail_rows, extent), bf16),
        ),
        scratch_shapes=[pltpu.SMEM((nbatch,), jnp.int32)],
        compiler_params=pltpu.CompilerParams(vmem_limit_bytes=4 * 1024 * 1024),
    )(owner_rows.reshape(-1), offsets.reshape(-1))


def sender(send_sem, recv_sem):
    def send(source, target, device, *index):
        copy = pltpu.make_async_remote_copy(
            src_ref=source, dst_ref=target,
            send_sem=send_sem.at[index] if index else send_sem,
            recv_sem=recv_sem.at[index] if index else recv_sem,
            device_id=device, device_id_type=pl.DeviceIdType.MESH,
        )
        copy.start()
        return copy

    return send


def places():
    nbatch, ntile = lax.axis_size("batch"), lax.axis_size("tile")
    at, col = lax.axis_index("batch"), lax.axis_index("tile")

    def along_batch(r):
        return (lax.rem(at + r, nbatch), col)

    def along_tile(r):
        return (at, lax.rem(col + r, ntile))

    return nbatch, ntile, at, col, along_batch, along_tile


def greet():
    nbatch, ntile, _, _, along_batch, along_tile = places()
    barrier = pltpu.get_barrier_semaphore()
    mesh_id = pl.DeviceIdType.MESH
    for r in range(1, nbatch):
        pl.semaphore_signal(barrier, inc=1, device_id=along_batch(r), device_id_type=mesh_id)
    for r in range(1, ntile):
        pl.semaphore_signal(barrier, inc=1, device_id=along_tile(r), device_id_type=mesh_id)
    return lambda: pl.semaphore_wait(barrier, nbatch - 1 + ntile - 1)


def greet_near():
    nbatch, ntile, _, _, along_batch, along_tile = places()
    barrier = pltpu.get_barrier_semaphore()
    mesh_id = pl.DeviceIdType.MESH
    near = (along_batch(1), along_batch(nbatch - 1), along_tile(1), along_tile(ntile - 1))
    for device in near:
        pl.semaphore_signal(barrier, inc=1, device_id=device, device_id_type=mesh_id)
    return lambda: pl.semaphore_wait(barrier, len(near))


def open_kernel(cap, index_ref, tails_ref, measured_ref, field_ref, sort_ref, *refs):
    nbatch, ntile, at, col, along_batch, along_tile = places()
    pays = refs[:nbatch]
    (
        got_ref, own_ref, other_ref, beside_ref, row_ref,
        pad, held, ready, edge, strip, beside, row_out, row_in, other, got,
        load_sem, pay_sem, tile_sem, edge_sem, row_sem,
    ) = refs[nbatch:]
    slices, _, height, width = field_ref.shape
    planes = 2 * slices
    positions, extent = held.shape[0], held.shape[-1]
    loads = [
        pltpu.make_async_copy(
            field_ref.at[q // 2, q % 2], pad.at[q, pl.ds(8, height), :], load_sem.at[q]
        )
        for q in range(planes)
    ] + [
        pltpu.make_async_copy(measured_ref.at[p], held.at[p], load_sem.at[planes + p])
        for p in range(positions)
    ]
    for load in loads:
        load.start()
    everyone_in = greet_near()
    for load in loads[:planes]:
        load.wait()
    lane = lax.broadcasted_iota(jnp.int32, (height, lanes), 1)
    edges = jnp.zeros((height, lanes), f32)
    for q in range(planes):
        edges = jnp.where(lane == q, pad[q, 8 : 8 + height, width - 1 : width], edges)
        edges = jnp.where(lane == planes + q, pad[q, 8 : 8 + height, 0:1], edges)
    edge[...] = edges.T[: edge.shape[0]]
    for q in range(planes):
        for j in range(width // lanes):
            cols = slice(j * lanes, (j + 1) * lanes)
            own_ref[q // 2, q % 2, j] = pad[q, 8 : 8 + height, cols].astype(bf16)
    everyone_in()
    send = sender(edge_sem.at[0], edge_sem.at[1])
    sides = [
        send(edge, strip.at[0], along_tile(1), 0),
        send(edge, strip.at[1], along_tile(ntile - 1), 1),
    ]
    sibling = (at + 1 - 2 * lax.rem(at, 2), col)
    tile_sent = sender(tile_sem.at[0], tile_sem.at[1])(own_ref, other, sibling)
    for load in loads[planes:]:
        load.wait()

    def arrange(p, carry):
        ready[p] = dot(held[p].astype(bf16), sort_ref[...]).astype(bf16)
        return carry

    lax.fori_loop(0, positions, arrange, 0)

    def fill(mask):
        for slot in range(cap):
            rows = slice(slot * extent, (slot + 1) * extent)
            pays[mask][rows] = ready[index_ref[mask * cap + slot]]
        pays[mask][cap * extent :] = tails_ref[mask]

    fill(1)
    pay_sent = sender(pay_sem.at[0], pay_sem.at[1])(pays[1], got, sibling)
    for copy in sides:
        copy.wait()
    blank = jnp.zeros((lanes - strip.shape[1], height), f32)
    for side in range(2):
        beside[side] = jnp.concatenate([strip[side], blank], 0).T
    for q in range(planes):
        first = beside[0, 0:1, q : q + 1]
        last = beside[1, height - 1 : height, planes + q : planes + q + 1]
        row_out[0, q : q + 1, :width] = pad[q, 8:9, :]
        row_out[0, q : q + 1, width:] = jnp.broadcast_to(first, (1, lanes))
        row_out[1, q : q + 1, :width] = pad[q, 7 + height : 8 + height, :]
        row_out[1, q : q + 1, width:] = jnp.broadcast_to(last, (1, lanes))
    send = sender(row_sem.at[0], row_sem.at[1])
    ends = [
        send(row_out.at[0], row_in.at[0], along_batch(nbatch - 1), 0),
        send(row_out.at[1], row_in.at[1], along_batch(1), 1),
    ]
    for mask in (0, *range(2, nbatch)):
        fill(mask)
    for copy in ends:
        copy.wait()
    beside_ref[...] = beside[...]
    row_ref[...] = row_in[...]
    tile_sent.wait()
    other_ref[...] = other[...]
    pay_sent.wait()
    got_ref[...] = got[...]


def open_up(cap, index, tails, intensities, field, sort):
    nbatch = lax.axis_size("batch")
    slices, _, height, width = field.shape
    planes = 2 * slices
    strip_rows = -(-2 * planes // 8) * 8
    positions, extent = intensities.shape[0], intensities.shape[-1]
    vmem = pl.BlockSpec(memory_space=pltpu.VMEM)
    anywhere = pl.BlockSpec(memory_space=pl.ANY)
    dma = pltpu.SemaphoreType.DMA
    tile = (slices, 2, width // lanes, height, lanes)
    pay = (cap * extent + tail_rows, extent)

    def kernel(*refs):
        open_kernel(cap, *refs)

    return pl.pallas_call(
        kernel,
        in_specs=[pl.BlockSpec(memory_space=pltpu.SMEM), vmem, anywhere, anywhere, vmem],
        out_specs=[vmem] * (nbatch + 5),
        out_shape=[jax.ShapeDtypeStruct(pay, bf16)] * (nbatch + 1)
        + [jax.ShapeDtypeStruct(tile, bf16)] * 2
        + [
            jax.ShapeDtypeStruct((2, height, lanes), f32),
            jax.ShapeDtypeStruct((2, 8, width + lanes), f32),
        ],
        scratch_shapes=[
            pltpu.VMEM((planes, height + 16, width), f32),
            pltpu.VMEM((positions, extent, extent), f32),
            pltpu.VMEM((positions, extent, extent), bf16),
            pltpu.VMEM((strip_rows, height), f32),
            pltpu.VMEM((2, strip_rows, height), f32),
            pltpu.VMEM((2, height, lanes), f32),
            pltpu.VMEM((2, 8, width + lanes), f32),
            pltpu.VMEM((2, 8, width + lanes), f32),
            pltpu.VMEM(tile, bf16),
            pltpu.VMEM(pay, bf16),
            dma((planes + positions,)),
            dma((2,)),
            dma((2,)),
            dma((2, 2)),
            dma((2, 2)),
        ],
        compiler_params=pltpu.CompilerParams(
            vmem_limit_bytes=40 * 1024 * 1024, collective_id=1, has_side_effects=True
        ),
    )(index, tails, intensities, field, sort)


def smooth_kernel(field_ref, beside, row_in, base_ref, pad, falls, rest):
    slices, _, height, width = field_ref.shape
    planes = 2 * slices
    for q in range(planes):
        pad[q, 8 : 8 + height, :] = field_ref[q // 2, q % 2]
    for q in range(planes):
        pad[q, 7:8, :] = row_in[1, q : q + 1, :width]
        pad[q, 8 + height : 9 + height, :] = row_in[0, q : q + 1, :width]

    def weighed(downs, rights):
        squares = sum(d * d for d in downs) + sum(d * d for d in rights)
        return lax.rsqrt(squares + tv_smooth)

    def flows(block):
        place = lax.broadcasted_iota(jnp.int32, (block, width), 1)
        for slab in range(slices):
            pair = (2 * slab, 2 * slab + 1)
            above = [pad[q, 7:8, :] for q in pair]
            corner = [row_in[1, q : q + 1, width : width + 1] for q in pair]
            downs = [pad[q, 8:9, :] - x for q, x in zip(pair, above)]
            rights = [
                jnp.where(place[:1] == width - 1, c, pltpu.roll(x, width - 1, 1)) - x
                for c, x in zip(corner, above)
            ]
            weight = weighed(downs, rights)
            for q, d in zip(pair, downs):
                falls[q, 7:8, :] = weight * d
            for start in range(0, height, block):
                here = [pad[q, 8 + start : 8 + start + block, :] for q in pair]
                below = [pad[q, 9 + start : 9 + start + block, :] for q in pair]
                edge_right = [
                    beside[1, start : start + block, planes + q : planes + q + 1] for q in pair
                ]
                downs = [b - x for b, x in zip(below, here)]
                rights = [
                    jnp.where(place == width - 1, e, pltpu.roll(x, width - 1, 1)) - x
                    for e, x in zip(edge_right, here)
                ]
                weight = weighed(downs, rights)
                left = [beside[0, start : start + block, q : q + 1] for q in pair]
                if start + block < height:
                    left_down = [beside[0, start + 1 : start + block + 1, q : q + 1] for q in pair]
                else:
                    left_down = [
                        jnp.concatenate(
                            [
                                beside[0, start + 1 : height, q : q + 1],
                                row_in[0, q : q + 1, width : width + 1],
                            ],
                            0,
                        )
                        for q in pair
                    ]
                left_rights = [x[:, :1] - l for x, l in zip(here, left)]
                left_weight = weighed([b - l for b, l in zip(left_down, left)], left_rights)
                for q, d, e, g in zip(pair, downs, rights, left_rights):
                    fall, run = weight * d, weight * e
                    before = jnp.where(place == 0, left_weight * g, pltpu.roll(run, 1, 1))
                    falls[q, 8 + start : 8 + start + block, :] = fall
                    rest[q, start : start + block, :] = before - run - fall

    flows(32)
    for q in range(planes):
        for j in range(width // lanes):
            cols = slice(j * lanes, (j + 1) * lanes)
            tv = falls[q, 7 : 7 + height, cols] + rest[q, :, cols]
            here = pad[q, 8 : 8 + height, cols]
            base_ref[q // 2, q % 2, :, cols] = here - update_rate * tv_weight * tv


def smooth(field, beside, row_in):
    slices, _, height, width = field.shape
    planes = 2 * slices
    vmem = pl.BlockSpec(memory_space=pltpu.VMEM)
    return pl.pallas_call(
        smooth_kernel,
        in_specs=[vmem] * 3,
        out_specs=vmem,
        out_shape=jax.ShapeDtypeStruct(field.shape, f32),
        scratch_shapes=[
            pltpu.VMEM((planes, height + 16, width), f32),
            pltpu.VMEM((planes, height + 8, width), f32),
            pltpu.VMEM((planes, height, width), f32),
        ],
        compiler_params=pltpu.CompilerParams(vmem_limit_bytes=24 * 1024 * 1024),
        cost_estimate=pl.CostEstimate(
            flops=60 * field.size, bytes_accessed=8 * field.size, transcendentals=field.size
        ),
    )(field, beside, row_in)


def finish_kernel(
    sums_ref, other_ref, total_ref, probe_ref, grad_ref, new_probe_ref,
    taken, mine, gathered, share, whole, sum_sem, gather_sem, share_sem, spread_sem,
):
    nbatch, ntile, at, col, along_batch, along_tile = places()
    extent = probe_ref.shape[-1]
    chunk = 2 * extent // nbatch
    everyone_in = greet()
    for part in range(2):
        mine[part * extent : (part + 1) * extent] = total_ref[part].astype(bf16)
    everyone_in()
    send = sender(gather_sem.at[0], gather_sem.at[1])
    gathers = []
    for r in range(1, nbatch):
        rows = pl.ds(lax.rem(at + r, nbatch) * chunk, chunk)
        gathers.append(send(mine.at[rows], gathered.at[r - 1], along_batch(r), r - 1))
    sibling = (at + 1 - 2 * lax.rem(at, 2), col)
    summed = sender(sum_sem.at[0], sum_sem.at[1])(other_ref, taken, sibling)
    for copy in gathers:
        copy.wait()
    part = mine[pl.ds(at * chunk, chunk)].astype(f32)
    for r in range(1, nbatch):
        part = part + gathered[r - 1].astype(f32)
    share[pl.ds(col, 1)] = part.astype(bf16)[None]
    send = sender(share_sem.at[0], share_sem.at[1])
    shares = [
        send(share.at[col], share.at[col], along_tile(r), r - 1) for r in range(1, ntile)
    ]
    summed.wait()
    slices, _, cols, _, _ = sums_ref.shape
    for slab in range(slices):
        for p in range(2):
            for j in range(cols):
                total = sums_ref[slab, p, j] + taken[slab, p, j].astype(f32)
                grad_ref[slab, p, :, j * lanes : (j + 1) * lanes] = total
    for copy in shares:
        copy.wait()
    final = share[0].astype(f32)
    for i in range(1, ntile):
        final = final + share[i].astype(f32)
    own_rows = pl.ds(at * chunk, chunk)
    whole[own_rows] = final.astype(bf16)
    send = sender(spread_sem.at[0], spread_sem.at[1])
    spreads = [
        send(whole.at[own_rows], whole.at[own_rows], along_batch(r), r - 1)
        for r in range(1, nbatch)
    ]
    for copy in spreads:
        copy.wait()
    for part in range(2):
        rows = slice(part * extent, (part + 1) * extent)
        new_probe_ref[part] = probe_ref[part].astype(f32) - probe_rate * whole[rows].astype(f32)


def finish(sums, other, total, probe, shape):
    nbatch, ntile = lax.axis_size("batch"), lax.axis_size("tile")
    extent = probe.shape[-1]
    chunk = 2 * extent // nbatch
    vmem = pl.BlockSpec(memory_space=pltpu.VMEM)
    dma = pltpu.SemaphoreType.DMA
    return pl.pallas_call(
        finish_kernel,
        in_specs=[vmem] * 4,
        out_specs=(vmem, vmem),
        out_shape=(
            jax.ShapeDtypeStruct(shape, f32),
            jax.ShapeDtypeStruct(probe.shape, f32),
        ),
        scratch_shapes=[
            pltpu.VMEM(other.shape, bf16),
            pltpu.VMEM((2 * extent, extent), bf16),
            pltpu.VMEM((nbatch - 1, chunk, extent), bf16),
            pltpu.VMEM((ntile, chunk, extent), bf16),
            pltpu.VMEM((2 * extent, extent), bf16),
            dma((2,)),
            dma((2, nbatch - 1)),
            dma((2, ntile - 1)),
            dma((2, nbatch - 1)),
        ],
        compiler_params=pltpu.CompilerParams(
            vmem_limit_bytes=20 * 1024 * 1024, collective_id=0, has_side_effects=True
        ),
        cost_estimate=pl.CostEstimate(
            flops=4 * sums.size, bytes_accessed=16 * sums.size, transcendentals=0
        ),
    )(sums, other, total, probe)


def on_device(object_field, probe_wave, intensities, owner_rows, offsets):
    extent = probe_wave.shape[-1]
    nbatch = lax.axis_size("batch")
    cap = max(2, 2 * intensities.shape[0] // nbatch)
    fixed = tables(extent)

    def swap(x, mask):
        return lax.ppermute(x, "batch", [(i, i ^ mask) for i in range(nbatch)])

    tabs, prop, sort = fixed
    index, tails = plan_slots(cap, owner_rows, offsets, extent)
    *pays, got, own, other, beside, row_in = open_up(
        cap, index, tails, intensities, object_field, sort
    )
    near = [swap(pays[m], m) for m in range(2, nbatch - 2)]

    def phase(group, carried, last=False):
        return visits(cap, group, own, other, probe_wave, (tabs, prop), carried, last)

    carried = phase((pays[0], got), ())
    base = smooth(object_field, beside, row_in)
    *carried, base, far_six, far_seven = lax.optimization_barrier(
        (*carried, base, pays[-2], pays[-1])
    )
    *near, far_six, far_seven = lax.optimization_barrier((*near, far_six, far_seven))
    far = [swap(far_six, nbatch - 2), swap(far_seven, nbatch - 1)]
    carried = phase(near, carried)
    carried = phase(far, carried, True)
    sums, returned, total = carried
    grad, new_probe = finish(sums, returned, total, probe_wave, object_field.shape)
    return (base - update_rate * grad, new_probe)


def solution(mesh):
    return jax.shard_map(
        on_device,
        mesh=mesh,
        in_specs=(
            P(None, None, "batch", "tile"),
            P(),
            P(("batch", "tile"), None, None),
            P(("batch", "tile"), None),
            P(("batch", "tile"), None),
        ),
        out_specs=(P(None, None, "batch", "tile"), P()),
        check_vma=False,
    )
```
